512 devices in a mesh: row: 32 (over z, x_lo), col: 16 (over x_hi, y, core).
Axes of the slice: x: 4 (x_hi: 2, x_lo: 2; x = x_hi * 2 + x_lo), y: 4, z: 16, core: 2. Of those that a mesh axis runs over, the one named last changes fastest.
Arguments:
- matrix: bfloat16 [8192, 24576], P('row', 'col'), may hold values from -6 to 6
- pivots: int32 [2, 256], replicated, may hold values from 256 to 8191, as said below
- lower_inverse: bfloat16 [2, 256, 256], replicated, as said below
- upper_inverse: bfloat16 [2, 256, 256], replicated, as said below
Outputs:
- factored: bfloat16 [8192, 24576], P('row', 'col')
The draws below stay inside these ranges and needn't reach their ends.
Inputs may be any that keep to these rules, and one draw needn't show every extreme that they name: Matrix row numbers (not stored rows). Within pivots[s] the entries are distinct and lie in (s + 1) * 256 .. 8191; each step lists (s + 1) * 256 and 8191. Each lower_inverse[s] has ones on the diagonal and zeros above it. Each upper_inverse[s] is zero below the diagonal.
All inputs are finite; a program needn't handle non-finite values.
Results may differ from the reference program's by a relative error of at most 0.0083.
Values may be sent and summed in bfloat16 or wider, within the bound.
A program may use at most 64 MiB of HBM per device.

```python
import jax
import jax.numpy as jnp
from jax import lax

B = 256
MR = 256
MC = 1536
NR = 8192
NC = 24576
N_ROW = 32
N_COL = 16


def draw_pivots(key, part):
    lists = []
    for step_index in range(2):
        subkey = jax.random.fold_in(key, 11 + step_index)
        lowest = (step_index + 1) * B
        extent = NR - lowest - 2
        ordered = jax.random.permutation(jax.random.fold_in(subkey, 1), extent)[:B - 2] + lowest + 1
        joined = jnp.concatenate([ordered.astype(jnp.int32), jnp.array([lowest, NR - 1], dtype=jnp.int32)])
        shuffled = jax.random.permutation(jax.random.fold_in(subkey, 2), joined)
        lists.append(shuffled.astype(jnp.int32))
    return jnp.stack(lists).astype(jnp.int32)


def draw_lower_inverse(key, part):
    subkey = jax.random.fold_in(key, 21)
    values = jax.random.normal(subkey, (2, B, B), jnp.float32)
    strict = jnp.tril(values, -1) / jnp.sqrt(jnp.float32(B))
    return (strict + jnp.eye(B, dtype=jnp.float32)[None]).astype(jnp.bfloat16)


def draw_upper_inverse(key, part):
    subkey = jax.random.fold_in(key, 31)
    values = jax.random.normal(subkey, (2, B, B), jnp.float32)
    strict = jnp.triu(values, 1) / jnp.sqrt(jnp.float32(B))
    diagonal = jnp.exp(jax.random.uniform(jax.random.fold_in(key, 32), (2, B), jnp.float32, -0.7, 0.7))
    whole = strict + diagonal[:, :, None] * jnp.eye(B, dtype=jnp.float32)[None]
    return (whole / jnp.sqrt(jnp.float32(B))).astype(jnp.bfloat16)


def levels(rng, dims, shards, smallest, high):
    gain = 1.0
    for dim, blocks in shards:
        heights = jax.random.uniform(jax.random.fold_in(jax.random.fold_in(rng, 6), dim), (blocks,), jnp.float32, smallest / len(shards), high / len(shards))
        gain = gain * jnp.repeat(jnp.exp(heights), dims[dim] // blocks).reshape((-1,) + (1,) * (len(dims) - 1 - dim))
    return gain


def gaussian(key, shape, spread, limit, split=(), kind=jnp.bfloat16):
    level = levels(key, shape, split, -0.22, 0.18) if split else 1.0
    values = jax.random.normal(key, shape, jnp.float32) * spread * level
    return jnp.minimum(jnp.maximum(values, -limit), limit).astype(kind)


def setup_inputs(seed: int = 0) -> dict:
    seeds = jax.random.split(jax.random.key(seed), 5)
    return {
        "matrix": gaussian(seeds[0], (NR, NC), 1.0, 6.0, ((0, 32), (1, 16))),
        "pivots": draw_pivots(jax.random.fold_in(seeds[4], 71), 0),
        "lower_inverse": draw_lower_inverse(jax.random.fold_in(seeds[4], 71), 0),
        "upper_inverse": draw_upper_inverse(jax.random.fold_in(seeds[4], 71), 0),
    }


def stored_rows(index):
    blocks = index // B
    return ((blocks % N_ROW) * MR + (blocks // N_ROW) * B + index % B).astype(jnp.int32)


def stored_cols(index):
    blocks = index // B
    return ((blocks % N_COL) * MC + (blocks // N_COL) * B + index % B).astype(jnp.int32)


def reference(matrix, pivots, lower_inverse, upper_inverse):
    row_ids = jnp.arange(NR, dtype=jnp.int32)
    col_ids = jnp.arange(NC, dtype=jnp.int32)
    row_block = ((row_ids % MR) // B) * N_ROW + row_ids // MR
    col_block = ((col_ids % MC) // B) * N_COL + col_ids // MC
    within = jnp.arange(B, dtype=jnp.int32)
    current = matrix
    for step_index in range(2):
        top_rows = stored_rows(step_index * B + within)
        pivot_rows = stored_rows(pivots[step_index].astype(jnp.int32))
        upper_block = current[top_rows]
        picked = current[pivot_rows]
        current = current.at[top_rows].set(picked).at[pivot_rows].set(upper_block)
        row_live = row_block > step_index
        col_live = col_block > step_index
        panel_cols = stored_cols(step_index * B + within)
        panel = jnp.take(current, panel_cols, axis=1).astype(jnp.float32)
        upper_inv = upper_inverse[step_index].astype(jnp.float32)
        lower_all = jnp.dot(panel, upper_inv, precision=lax.Precision.HIGHEST).astype(matrix.dtype)
        lower_all = jnp.where(row_live[:, None], lower_all, jnp.zeros_like(lower_all))
        new_top = current[top_rows].astype(jnp.float32)
        lower_inv = lower_inverse[step_index].astype(jnp.float32)
        upper = jnp.dot(lower_inv, new_top, precision=lax.Precision.HIGHEST).astype(matrix.dtype)
        upper = jnp.where(col_live[None, :], upper, jnp.zeros_like(upper))
        upper_wide = upper.astype(jnp.float32)

        def update(pair):
            rows_here, lower_here = pair
            product = jnp.dot(lower_here.astype(jnp.float32), upper_wide, precision=lax.Precision.HIGHEST)
            return (rows_here.astype(jnp.float32) - product).astype(matrix.dtype)

        stacked = lax.map(update, (current.reshape(N_ROW, MR, NC), lower_all.reshape(N_ROW, MR, B)))
        current = stacked.reshape(NR, NC)
        old_panel = jnp.take(current, panel_cols, axis=1)
        current = current.at[:, panel_cols].set(jnp.where(row_live[:, None], lower_all, old_panel))
        old_top = current[top_rows]
        current = current.at[top_rows].set(jnp.where(col_live[None, :], upper, old_top))
    return current
```

```python
import functools

import jax
import jax.numpy as jnp
from jax import lax
from jax.experimental import pallas as pl
from jax.experimental.pallas import tpu as pltpu
from jax.sharding import PartitionSpec as P

MESH = pl.DeviceIdType.MESH
F32 = jnp.float32
BF16 = jnp.bfloat16
SUB = 3


def dot(a, b):
    return jnp.dot(a, b, preferred_element_type=F32)


def kernel(
    rows_n, cols_n,
    a_ref, piv_ref, lo_ref, up_ref, o_ref,
    cand, rp, rm, fin, xb, tb, te, db, de, pb, gsel, own_ref,
    rp_s, rp_r, rm_s, rm_r, x_s, x_r, e_s, e_r,
    tp_s, tp_r, tx_s, tx_r, dp_s, dp_r, dx_s, dx_r,
    pan_s, pan_r, sc_s, sc_r,
):
    block = lo_ref.shape[1]
    zn = rows_n // 2
    half = zn // 2
    width = cand.shape[-1]
    per = block // zn
    row = lax.axis_index("row")
    col = lax.axis_index("col")
    z = row // 2
    xl = lax.rem(row, 2)
    up_id = (lax.rem(row + 2, rows_n), col)
    down_id = (lax.rem(row + rows_n - 2, rows_n), col)
    pair_id = (row + 1 - 2 * xl, col)
    is_root = z == 0
    home = lambda k: lax.rem(k + 4 * zn, zn)

    barrier = pltpu.get_barrier_semaphore()
    for dest in (up_id, down_id, pair_id):
        pl.semaphore_signal(barrier, inc=1, device_id=dest, device_id_type=MESH)
    for p in range(2):
        @pl.when(col != p)
        def _():
            pl.semaphore_signal(barrier, inc=1, device_id=(row, p), device_id_type=MESH)

    @pl.when(z != 0)
    def _():
        pl.semaphore_signal(barrier, inc=1, device_id=(xl, col), device_id_type=MESH)

    base = (row * block).astype(F32)
    ii = lax.broadcasted_iota(jnp.int32, (block, block), 0).astype(F32)
    jj = lax.broadcasted_iota(jnp.int32, (block, block), 1).astype(F32)
    p0r = piv_ref[0:1, :].astype(F32)
    p1r = piv_ref[1:2, :].astype(F32)
    eye = ii == jj
    p0c = jnp.sum(jnp.where(eye, p0r, 0.0), axis=1, keepdims=True)
    p1c = jnp.sum(jnp.where(eye, p1r, 0.0), axis=1, keepdims=True)
    q1c = p1c + jnp.sum(jnp.where(p1c == p0r, jj - p1c, 0.0), axis=1, keepdims=True)
    sel0 = jnp.where(p0c == base + jj, 1.0, 0.0).astype(BF16)
    sel1 = jnp.where(q1c == base + jj, 1.0, 0.0).astype(BF16)
    for s in range(SUB):
        a_s = a_ref[:, s * width : (s + 1) * width]
        cand[s, :, 0] = dot(sel0, a_s).astype(BF16).reshape(zn, per, width)
        cand[s, :, 1] = dot(sel1, a_s).astype(BF16).reshape(zn, per, width)

    h0 = jnp.where(base + ii == p0r, 1.0, 0.0)
    h1 = jnp.where(base + ii == p1r, 1.0, 0.0)
    any0 = jnp.sum(h0, axis=1, keepdims=True)
    any1 = jnp.sum(h1, axis=1, keepdims=True)
    into1 = jnp.where(p0r == block + ii, 1.0, 0.0)
    from0 = jnp.sum(jnp.where(p0c == block + jj, 1.0, 0.0), axis=0, keepdims=True)
    via = dot(h1.astype(BF16), into1.astype(BF16))
    gsel[:, 0:block] = (via + h0 * (1.0 - any1)).astype(BF16)
    gsel[:, block : 2 * block] = (h1 * (1.0 - from0)).astype(BF16)
    own_ref[...] = jnp.broadcast_to((1.0 - any1) * (1.0 - any0), own_ref.shape)

    waits = 3 + jnp.where(col < 2, cols_n - 1, 0) + jnp.where(is_root, zn - 1, 0)
    pl.semaphore_wait(barrier, waits)

    def remote(src, dst, ssem, rsem, dest):
        return pltpu.make_async_remote_copy(
            src_ref=src, dst_ref=dst, send_sem=ssem, recv_sem=rsem,
            device_id=dest, device_id_type=MESH,
        )

    def panel_copy(p, other):
        return remote(
            a_ref.at[:, pl.ds(0, block)], pb.at[:, pl.ds(p * block, block)],
            pan_s.at[other], pan_r.at[p], (row, other),
        )

    def panel(p, action):
        @pl.when(col == p)
        def _():
            for other in range(cols_n):
                if other != p:
                    action(panel_copy(p, other))

    for p in range(2):
        panel(p, lambda c: c.start())

        @pl.when(col == p)
        def _():
            pb[:, p * block : (p + 1) * block] = a_ref[:, 0:block]

    def scatter_main(k):
        return remote(
            a_ref.at[pl.ds(k * per, per)], db.at[xl, k], sc_s.at[0, k], sc_r.at[0],
            (2 * k + xl, col),
        )

    def scatter_ext(k):
        return remote(
            pb.at[pl.ds(k * per, per)], de.at[xl, k], sc_s.at[1, k], sc_r.at[1],
            (2 * k + xl, col),
        )

    def plus(t, s):
        src = cand.at[s, home(z + half)] if t == 0 else rp.at[t - 1, s]
        return remote(src, rp.at[t, s], rp_s.at[t, s], rp_r.at[t, s], up_id)

    def minus(t, s):
        src = cand.at[s, home(z - half + 1)] if t == 0 else rm.at[t - 1, s]
        return remote(src, rm.at[t, s], rm_s.at[t, s], rm_r.at[t, s], down_id)

    for s in range(SUB):
        plus(0, s).start()
        minus(0, s).start()

    @pl.when(is_root)
    def _():
        for k in range(1, zn):
            scatter_main(k).start()
        db[xl, 0] = a_ref[0:per, :]

    for t in range(1, half):
        for s in range(SUB):
            plus(t - 1, s).wait_recv()
            rp[t - 1, s] = rp[t - 1, s] + cand[s, home(z + half - t)]
            plus(t, s).start()
            if t < half - 1:
                minus(t - 1, s).wait_recv()
                rm[t - 1, s] = rm[t - 1, s] + cand[s, home(z - half + 1 + t)]
                minus(t, s).start()
        if t == half // 2:
            for p in range(2):
                @pl.when(col != p)
                def _():
                    panel_copy(p, 0).wait_recv()

            @pl.when(is_root)
            def _():
                for k in range(1, zn):
                    scatter_ext(k).start()
                de[xl, 0] = pb[0:per, :]

    def swap(s):
        return remote(fin.at[s, 1 - xl], xb.at[s], x_s.at[s], x_r.at[s], pair_id)

    for s in range(SUB):
        plus(half - 1, s).wait_recv()
        minus(half - 2, s).wait_recv()
        fin[s] = cand[s, z] + rp[half - 1, s] + rm[half - 2, s]
        swap(s).start()
    for s in range(SUB):
        swap(s).wait_recv()
        tb[xl, s, z] = fin[s, xl] + xb[s]

    source = 1 - xl

    def ext_copy(other):
        return remote(
            tb.at[xl, 0, z, :, pl.ds(0, block)], te.at[xl, z], e_s.at[other], e_r, (row, other)
        )

    for p in range(2):
        @pl.when(jnp.logical_and(col == p, source == p))
        def _():
            for other in range(cols_n):
                if other != p:
                    ext_copy(other).start()
            te[xl, z] = tb[xl, 0, z, :, 0:block]

    @pl.when(z != 0)
    def _():
        scatter_main(1).wait_recv()
        scatter_ext(1).wait_recv()

    n_t, n_d = SUB + 1, 2

    def t_piece(part, j, k):
        return tb.at[part, j, k] if j < SUB else te.at[part, k]

    def d_piece(part, j, k):
        return db.at[part, k] if j == 0 else de.at[part, k]

    def along(piece, ssem, rsem, d, t, j):
        k = home(z - t) if d == 0 else home(z + t)
        ref = piece(xl, j, k)
        slot = t if d == 0 else half + t
        return remote(ref, ref, ssem.at[slot, j], rsem.at[slot, j], up_id if d == 0 else down_id)

    def across(piece, ssem, rsem, d, t, j):
        k = home(z - t) if d == 0 else home(z + t)
        ref = piece(xl, j, k)
        slot = t if d == 0 else half + t
        return remote(ref, ref, ssem.at[slot, j], rsem.at[slot, j], pair_id)

    streams = ((t_piece, n_t, tp_s, tp_r, tx_s, tx_r), (d_piece, n_d, dp_s, dp_r, dx_s, dx_r))

    def not_source(action):
        @pl.when(col != source)
        def _():
            action()

    for t in range(half + 1):
        for piece, n, ps, pr, xs, xr in streams:
            for j in range(n):
                if t == 0:
                    if piece is t_piece and j == SUB:
                        not_source(lambda: ext_copy(0).wait_recv())
                    for d in range(2):
                        along(piece, ps, pr, d, 0, j).start()
                    across(piece, xs, xr, 0, 0, j).start()
                else:
                    for d in range(2):
                        if d == 0 or t < half:
                            along(piece, ps, pr, d, t - 1, j).wait_recv()
                            if t < (half if d == 0 else half - 1):
                                along(piece, ps, pr, d, t, j).start()
                            across(piece, xs, xr, d, t, j).start()
    for piece, n, ps, pr, xs, xr in streams:
        for j in range(n):
            for t in range(half + 1):
                across(piece, xs, xr, 0, t, j).wait_recv()
                if 0 < t < half:
                    across(piece, xs, xr, 1, t, j).wait_recv()

    lo0, lo1, up0, up1 = lo_ref[0], lo_ref[1], up_ref[0], up_ref[1]
    ext0 = te[0].reshape(block, block)
    ext1 = te[1].reshape(block, block)
    lower_t = dot(ext1, up0).astype(BF16)

    def top(s):
        t0 = tb[0, s].reshape(block, width)
        t1 = tb[1, s].reshape(block, width)
        u0 = dot(lo0, t0).astype(BF16)
        return t0, t1, u0

    def second(t1, u0):
        t1u = (t1.astype(F32) - dot(lower_t, u0)).astype(BF16)
        return t1u, dot(lo1, t1u).astype(BF16)

    def cols(s):
        return slice(s * width, (s + 1) * width)

    @pl.when(row == 0)
    def _():
        for s in range(SUB):
            t0, _, u0 = top(s)
            o_ref[:, cols(s)] = u0

        @pl.when(col == 0)
        def _():
            o_ref[:, 0:block] = tb[0, 0].reshape(block, width)[:, 0:block]

    @pl.when(row == 1)
    def _():
        for s in range(SUB):
            _, t1, u0 = top(s)
            t1u, u1 = second(t1, u0)
            o_ref[:, cols(s)] = u1
            if s == 0:
                @pl.when(col == 1)
                def _():
                    o_ref[:, 0:block] = t1u[:, 0:block]

        @pl.when(col == 0)
        def _():
            o_ref[:, 0:block] = lower_t

    @pl.when(row > 1)
    def _():
        own = own_ref[:, 0:1]
        g = gsel[...]
        moved = jnp.concatenate([de[0].reshape(block, 2 * block), de[1].reshape(block, 2 * block)], axis=0)
        pan = dot(g, moved) + own * pb[...].astype(F32)
        l0 = dot(pan[:, 0:block].astype(BF16), up0).astype(BF16)
        u0e = dot(lo0, ext0).astype(BF16)
        y1 = (pan[:, block : 2 * block] - dot(l0, u0e)).astype(BF16)
        l1 = dot(y1, up1).astype(BF16)
        ll = jnp.concatenate([l0, l1], axis=1)
        for s in range(SUB):
            _, t1, u0 = top(s)
            _, u1 = second(t1, u0)
            d0 = db[0, :, :, cols(s)].reshape(block, width)
            d1 = db[1, :, :, cols(s)].reshape(block, width)
            x = dot(g, jnp.concatenate([d0, d1], axis=0)) + own * a_ref[:, cols(s)].astype(F32)
            uu = jnp.concatenate([u0, u1], axis=0)
            o_ref[:, cols(s)] = (x - dot(ll, uu)).astype(BF16)

        @pl.when(col == 0)
        def _():
            o_ref[:, 0:block] = l0

        @pl.when(col == 1)
        def _():
            o_ref[:, 0:block] = l1

    for p in range(2):
        panel(p, lambda c: c.wait_send())

    @pl.when(is_root)
    def _():
        for k in range(1, zn):
            scatter_main(k).wait_send()
            scatter_ext(k).wait_send()

    for s in range(SUB):
        for t in range(half):
            plus(t, s).wait_send()
            if t < half - 1:
                minus(t, s).wait_send()
        swap(s).wait_send()
    for p in range(2):
        @pl.when(jnp.logical_and(col == p, source == p))
        def _():
            for other in range(cols_n):
                if other != p:
                    ext_copy(other).wait_send()

    for piece, n, ps, pr, xs, xr in streams:
        for j in range(n):
            for t in range(half + 1):
                across(piece, xs, xr, 0, t, j).wait_send()
                if 0 < t < half:
                    across(piece, xs, xr, 1, t, j).wait_send()
                if t < half:
                    along(piece, ps, pr, 0, t, j).wait_send()
                if t < half - 1:
                    along(piece, ps, pr, 1, t, j).wait_send()


def body(matrix, pivots, lower_inverse, upper_inverse):
    local_rows, local_cols = matrix.shape
    block = lower_inverse.shape[1]
    rows_n = lax.axis_size("row")
    cols_n = lax.axis_size("col")
    zn = rows_n // 2
    half = zn // 2
    per = block // zn
    width = local_cols // SUB
    sem = pltpu.SemaphoreType.DMA
    vmem = pltpu.VMEM
    return pl.pallas_call(
        functools.partial(kernel, rows_n, cols_n),
        out_shape=jax.ShapeDtypeStruct((local_rows, local_cols), BF16),
        in_specs=[pl.BlockSpec(memory_space=pltpu.VMEM)] * 4,
        out_specs=pl.BlockSpec(memory_space=pltpu.VMEM),
        scratch_shapes=[
            vmem((SUB, zn, 2, per, width), BF16),
            vmem((half, SUB, 2, per, width), BF16),
            vmem((half - 1, SUB, 2, per, width), BF16),
            vmem((SUB, 2, per, width), BF16),
            vmem((SUB, per, width), BF16),
            vmem((2, SUB, zn, per, width), BF16),
            vmem((2, zn, per, block), BF16),
            vmem((2, zn, per, local_cols), BF16),
            vmem((2, zn, per, 2 * block), BF16),
            vmem((block, 2 * block), BF16),
            vmem((block, 2 * block), BF16),
            vmem((block, 128), F32),
            sem((half, SUB)), sem((half, SUB)),
            sem((half - 1, SUB)), sem((half - 1, SUB)),
            sem((SUB,)), sem((SUB,)),
            sem((cols_n,)), sem(()),
            sem((2 * half - 1, SUB + 1)), sem((2 * half - 1, SUB + 1)),
            sem((2 * half, SUB + 1)), sem((2 * half, SUB + 1)),
            sem((2 * half - 1, 2)), sem((2 * half - 1, 2)),
            sem((2 * half, 2)), sem((2 * half, 2)),
            sem((cols_n,)), sem((2,)),
            sem((2, zn)), sem((2,)),
        ],
        compiler_params=pltpu.CompilerParams(
            collective_id=0, has_side_effects=True, vmem_limit_bytes=56 << 20
        ),
    )(matrix, pivots, lower_inverse, upper_inverse)


def solution(mesh):
    placed = (P("row", "col"), P(), P(), P())
    return jax.shard_map(
        body, mesh=mesh, in_specs=placed, out_specs=P("row", "col"), check_vma=False
    )
```

```python
import functools

import jax
import jax.numpy as jnp
from jax import lax
from jax.experimental import pallas as pl
from jax.experimental.pallas import tpu as pltpu
from jax.sharding import PartitionSpec as P

MESH = pl.DeviceIdType.MESH
F32 = jnp.float32
BF16 = jnp.bfloat16
SUB = 3
T_HOP = 2
D_HOP = 2
FULL = 0
D_START = 2
PAN_A = 0
PAN_X = 2
PAN_B = 3
DO_D = True
DO_COMP = True
DO_T = True
DO_PAN = True
D_CROSS = True
SC_N = 15
SC_0 = 0


def dot(a, b):
    return jnp.dot(a, b, preferred_element_type=F32)


def kernel(
    rows_n, cols_n,
    a_ref, piv_ref, lo_ref, up_ref, o_ref,
    cand, lead, selh, rp, rm, fin, xb, tb, te, db, pb, gsel, own_ref,
    rp_s, rp_r, rm_s, rm_r, x_s, x_r, e_s, e_r,
    tp_s, tp_r, tx_s, tx_r, dp_s, dp_r, dx_s, dx_r,
    pan_s, pan_r, sc_s, sc_r,
):
    block = lo_ref.shape[1]
    zn = rows_n // 2
    half = zn // 2
    width = cand.shape[-1]
    per = block // zn
    row = lax.axis_index("row")
    col = lax.axis_index("col")
    z = row // 2
    xl = lax.rem(row, 2)
    core = lax.rem(col, 2)
    pair_id = (row + 1 - 2 * xl, col)
    core_id = (row, col + 1 - 2 * core)
    is_root = z == 0
    source = 1 - xl

    def home(k):
        return lax.rem(k + 4 * zn, zn)

    def at_z(i):
        return (2 * home(z + i) + xl, col)

    barrier = pltpu.get_barrier_semaphore()

    def greet(dest):
        pl.semaphore_signal(barrier, inc=1, device_id=dest, device_id_type=MESH)

    reach = max(T_HOP, D_HOP)
    for i in range(1, reach + 1):
        greet(at_z(i))
        greet(at_z(-i))
    greet(pair_id)
    greet(core_id)
    for p in range(2):
        @pl.when(col != p)
        def _():
            greet((row, p))

    @pl.when(col > cols_n // 2 + 1)
    def _():
        greet((row, cols_n // 2 + core))

    @pl.when(z != 0)
    def _():
        greet((xl, col))

    base = (row * block).astype(F32)
    ii = lax.broadcasted_iota(jnp.int32, (block, block), 0).astype(F32)
    jj = lax.broadcasted_iota(jnp.int32, (block, block), 1).astype(F32)
    p0r = piv_ref[0:1, :].astype(F32)
    p1r = piv_ref[1:2, :].astype(F32)
    eye = ii == jj
    p0c = jnp.sum(jnp.where(eye, p0r, 0.0), axis=1, keepdims=True)
    p1c = jnp.sum(jnp.where(eye, p1r, 0.0), axis=1, keepdims=True)
    q1c = p1c + jnp.sum(jnp.where(p1c == p0r, jj - p1c, 0.0), axis=1, keepdims=True)
    selh[:, 0] = jnp.where(p0c == base + jj, 1.0, 0.0).astype(BF16).reshape(zn, per, block)
    selh[:, 1] = jnp.where(q1c == base + jj, 1.0, 0.0).astype(BF16).reshape(zn, per, block)
    firsts = (home(z + half), home(z - half + 1))
    for d in range(2):
        sel = selh[firsts[d]].reshape(2 * per, block)
        for s in range(SUB):
            part = dot(sel, a_ref[:, s * width : (s + 1) * width]).astype(BF16)
            lead[d, s] = part.reshape(2, per, width)

    waits = 2 * reach + 2 + jnp.where(col < 2, cols_n - 1, 0) + jnp.where(col // 2 == cols_n // 4, cols_n // 4 - 1, 0) + jnp.where(is_root, zn - 1, 0)
    pl.semaphore_wait(barrier, waits)

    def remote(src, dst, ssem, rsem, dest):
        return pltpu.make_async_remote_copy(
            src_ref=src, dst_ref=dst, send_sem=ssem, recv_sem=rsem,
            device_id=dest, device_id_type=MESH,
        )

    def plus(t, s):
        src = lead.at[0, s] if t == 0 else rp.at[t - 1, s]
        return remote(src, rp.at[t, s], rp_s.at[t, s], rp_r.at[t, s], at_z(1))

    def minus(t, s):
        src = lead.at[1, s] if t == 0 else rm.at[t - 1, s]
        return remote(src, rm.at[t, s], rm_s.at[t, s], rm_r.at[t, s], at_z(-1))

    def reduce_step(t):
        for s in range(SUB):
            if t == 0:
                plus(0, s).start()
                minus(0, s).start()
                continue
            plus(t - 1, s).wait_recv()
            rp[t - 1, s] = rp[t - 1, s] + cand[s, home(z + half - t)]
            plus(t, s).start()
            if t < half - 1:
                minus(t - 1, s).wait_recv()
                rm[t - 1, s] = rm[t - 1, s] + cand[s, home(z - half + 1 + t)]
                minus(t, s).start()

    def candidates():
        for s in range(SUB):
            sel = selh[...].reshape(zn * 2 * per, block)
            part = dot(sel, a_ref[:, s * width : (s + 1) * width]).astype(BF16)
            cand[s] = part.reshape(zn, 2, per, width)

    def sources():
        h0 = jnp.where(base + ii == p0r, 1.0, 0.0)
        h1 = jnp.where(base + ii == p1r, 1.0, 0.0)
        any0 = jnp.sum(h0, axis=1, keepdims=True)
        any1 = jnp.sum(h1, axis=1, keepdims=True)
        into1 = jnp.where(p0r == block + ii, 1.0, 0.0)
        from0 = jnp.sum(jnp.where(p0c == block + jj, 1.0, 0.0), axis=0, keepdims=True)
        via = dot(h1.astype(BF16), into1.astype(BF16))
        gsel[:, 0:block] = (via + h0 * (1.0 - any1)).astype(BF16)
        gsel[:, block : 2 * block] = (h1 * (1.0 - from0)).astype(BF16)
        own_ref[...] = jnp.broadcast_to((1.0 - any1) * (1.0 - any0), own_ref.shape)

    def panel_copy(p, other):
        return remote(pb.at[p], pb.at[p], pan_s.at[other], pan_r.at[p], (row, other))

    far = cols_n // 2

    def panel_far(action):
        for p in range(2):
            @pl.when(col == p)
            def _():
                action(panel_copy(p, far + p))

    def panel_near(action, first):
        for p in range(2):
            @pl.when(col == first + p)
            def _():
                for other in range(2, far, 2):
                    action(panel_copy(p, first + p + other))

    def core_copy(p):
        return remote(pb.at[p], pb.at[p], pan_s.at[0], pan_r.at[p], core_id)

    def panel_start():
        @pl.when(col == 0)
        def _():
            pb[0] = dot(o_ref[:, 0:block], up_ref[0]).astype(BF16)

        @pl.when(col == 1)
        def _():
            pb[1] = o_ref[:, 0:block]

        panel_far(lambda c: c.start())
        panel_near(lambda c: c.start(), 0)

    def panel_relay():
        for p in range(2):
            @pl.when(col == far + p)
            def _():
                panel_copy(p, far + p).wait_recv()

        panel_near(lambda c: c.start(), far)

    def panel_pass():
        for p in range(2):
            @pl.when(core == p)
            def _():
                @pl.when(lax.rem(col, far) != p)
                def _():
                    core_copy(p).wait_recv()

                core_copy(p).start()

    def panel_wait():
        for p in range(2):
            @pl.when(core != p)
            def _():
                core_copy(p).wait_recv()

    order = [k if i == 0 else zn - k for k in range(half, 0, -1) for i in range(2) if k < half or i == 0]

    def scatter_main(k):
        return remote(
            a_ref.at[pl.ds(k * per, per)], db.at[xl, k], sc_s.at[k], sc_r,
            (2 * k + xl, col),
        )

    def scatter_start(t):
        @pl.when(is_root)
        def _():
            for k in order[SC_N * t : SC_N * t + SC_N]:
                scatter_main(k).start()
            if t == 0:
                db[xl, 0] = a_ref[0:per, :]

    def scatter_wait():
        @pl.when(z != 0)
        def _():
            scatter_main(1).wait_recv()

    def t_piece(part, j, k):
        if j == 0:
            return te.at[part, k]
        return tb.at[:, j - 1, k] if j <= FULL else tb.at[part, j - 1, k]

    def d_piece(part, j, k):
        return db.at[part, k]

    t_stream = (t_piece, SUB + 1, T_HOP, tp_s, tp_r, tx_s, tx_r)
    d_stream = (d_piece, 1, D_HOP, dp_s, dp_r, dx_s, dx_r)

    def crosses(stream, j):
        if not D_CROSS and stream is d_stream:
            return False
        return stream is d_stream or j == 0 or j > FULL

    def along(stream, d, m, j, sender):
        piece, _, hop, ssem, rsem, _, _ = stream
        i = (m - 1) % hop + 1
        back = m - i if sender else m
        sign = 1 if d == 0 else -1
        ref = piece(xl, j, home(z - sign * back))
        slot = m if d == 0 else half + m
        return remote(ref, ref, ssem.at[slot, j], rsem.at[slot, j], at_z(sign * i))

    def across(stream, d, m, j):
        piece, _, _, _, _, ssem, rsem = stream
        ref = piece(xl, j, home(z - m if d == 0 else z + m))
        slot = m if d == 0 else half + m
        return remote(ref, ref, ssem.at[slot, j], rsem.at[slot, j], pair_id)

    def across_other(stream, d, m, j):
        piece, _, _, _, _, ssem, rsem = stream
        ref = piece(1 - xl, j, home(z - m if d == 0 else z + m))
        slot = m if d == 0 else half + m
        return remote(ref, ref, ssem.at[slot, j], rsem.at[slot, j], pair_id)

    last = (half, half - 1)

    def send_from(stream, d, u, j):
        hop = stream[2]
        for m in range(hop * u + 1, min(hop * u + hop, last[d]) + 1):
            along(stream, d, m, j, True).start()

    def gather_step(stream, u, js):
        hop = stream[2]
        for j in js:
            if u == 0:
                for d in range(2):
                    send_from(stream, d, 0, j)
                if crosses(stream, j):
                    across(stream, 0, 0, j).start()
        if u == 0:
            return
        for i in range(hop, 0, -1):
            m = hop * (u - 1) + i
            for j in js:
                for d in range(2):
                    if m <= last[d]:
                        along(stream, d, m, j, False).wait_recv()
                        if i == hop:
                            send_from(stream, d, u, j)
            for j in js:
                for d in range(2):
                    if m <= last[d] and crosses(stream, j):
                        across(stream, d, m, j).start()

    def steps(stream):
        return -(-half // stream[2]) + 1

    def slots():
        yield 0, 0
        for d in range(2):
            for m in range(1, last[d] + 1):
                yield d, m

    def cross_wait(stream):
        for j in range(stream[1]):
            for d, m in slots():
                if crosses(stream, j):
                    across_other(stream, d, m, j).wait_recv()

    def gather_sent(stream):
        for j in range(stream[1]):
            for d, m in slots():
                if crosses(stream, j):
                    across(stream, d, m, j).wait_send()
                if m:
                    along(stream, d, m, j, True).wait_send()

    def swap(s):
        if s < FULL:
            return remote(fin.at[s], xb.at[s], x_s.at[s], x_r.at[s], pair_id)
        return remote(fin.at[s, 1 - xl], xb.at[s, 0], x_s.at[s], x_r.at[s], pair_id)

    def swap_start():
        for s in range(SUB):
            plus(half - 1, s).wait_recv()
            minus(half - 2, s).wait_recv()
            fin[s] = cand[s, z] + rp[half - 1, s] + rm[half - 2, s]
            swap(s).start()

    def swap_wait(s):
        swap(s).wait_recv()
        if s < FULL:
            tb[:, s, z] = fin[s] + xb[s]
        else:
            tb[xl, s, z] = fin[s, xl] + xb[s, 0]

    def ext_copy(other):
        return remote(
            tb.at[xl, 0, z, :, pl.ds(0, block)], te.at[xl, z], e_s.at[other], e_r, (row, other)
        )

    def ext(action):
        for p in range(2):
            @pl.when(jnp.logical_and(col == p, source == p))
            def _():
                for other in range(cols_n):
                    if other != p:
                        action(ext_copy(other))

    def ext_start():
        ext(lambda c: c.start())

        @pl.when(col == source)
        def _():
            te[xl, z] = tb[xl, 0, z, :, 0:block]

    def ext_wait():
        @pl.when(col != source)
        def _():
            ext_copy(0).wait_recv()

    def cols(s):
        return slice(s * width, (s + 1) * width)

    def exchanged():
        own = own_ref[:, 0:1]
        g = gsel[...]
        for s in range(SUB):
            d0 = db[0, :, :, cols(s)].reshape(block, width)
            d1 = db[1, :, :, cols(s)].reshape(block, width)
            x = dot(g, jnp.concatenate([d0, d1], axis=0)) + own * a_ref[:, cols(s)].astype(F32)
            o_ref[:, cols(s)] = x.astype(BF16)

    d_next = [0]

    def d_step():
        if DO_D and d_next[0] < steps(d_stream):
            if d_next[0] == 0:
                scatter_wait()
            gather_step(d_stream, d_next[0], (0,))
            d_next[0] += 1

    reduce_step(0)
    if DO_D and SC_0 == 0:
        scatter_start(0)
    candidates()
    sources()
    for t in range(1, half):
        reduce_step(t)
        if DO_D and t >= SC_0:
            scatter_start(t - SC_0)
        if t >= D_START:
            d_step()
    swap_start()
    d_step()

    def panel_point(u):
        if DO_D and u == PAN_A:
            while d_next[0] < steps(d_stream):
                d_step()
            if D_CROSS:
                cross_wait(d_stream)
            exchanged()
            if DO_PAN:
                panel_start()
        if DO_PAN and DO_D and u == PAN_X:
            panel_relay()
        if DO_PAN and DO_D and u == PAN_B:
            panel_pass()

    panel_point(-1)
    swap_wait(0)
    ext_start()
    for s in range(1, SUB):
        swap_wait(s)
    main = tuple(range(1, SUB + 1))
    if DO_T:
        gather_step(t_stream, 0, main)
    panel_point(0)
    ext_wait()
    if DO_T:
        gather_step(t_stream, 0, (0,))
        for u in range(1, steps(t_stream)):
            gather_step(t_stream, u, main + (0,))
            panel_point(u)
        cross_wait(t_stream)
    if DO_D and DO_PAN:
        panel_wait()

    lo0, lo1, up0, up1 = lo_ref[0], lo_ref[1], up_ref[0], up_ref[1]

    if DO_COMP:
        ext0 = te[0].reshape(block, block)
        ext1 = te[1].reshape(block, block)
        lower_t = dot(ext1, up0).astype(BF16)

        def top(s):
            t0 = tb[0, s].reshape(block, width)
            t1 = tb[1, s].reshape(block, width)
            return t0, t1, dot(lo0, t0).astype(BF16)

        def second(t1, u0):
            t1u = (t1.astype(F32) - dot(lower_t, u0)).astype(BF16)
            return t1u, dot(lo1, t1u).astype(BF16)

        @pl.when(row == 0)
        def _():
            for s in range(SUB):
                o_ref[:, cols(s)] = top(s)[2]

            @pl.when(col == 0)
            def _():
                o_ref[:, 0:block] = tb[0, 0].reshape(block, width)[:, 0:block]

        @pl.when(row == 1)
        def _():
            for s in range(SUB):
                _, t1, u0 = top(s)
                t1u, u1 = second(t1, u0)
                o_ref[:, cols(s)] = u1
                if s == 0:
                    @pl.when(col == 1)
                    def _():
                        o_ref[:, 0:block] = t1u[:, 0:block]

            @pl.when(col == 0)
            def _():
                o_ref[:, 0:block] = lower_t

        @pl.when(row > 1)
        def _():
            l0 = pb[0]
            u0e = dot(lo0, ext0).astype(BF16)
            y1 = (pb[1].astype(F32) - dot(l0, u0e)).astype(BF16)
            l1 = dot(y1, up1).astype(BF16)
            ll = jnp.concatenate([l0, l1], axis=1)
            for s in range(SUB):
                _, t1, u0 = top(s)
                _, u1 = second(t1, u0)
                uu = jnp.concatenate([u0, u1], axis=0)
                o_ref[:, cols(s)] = (o_ref[:, cols(s)].astype(F32) - dot(ll, uu)).astype(BF16)

            @pl.when(col == 0)
            def _():
                o_ref[:, 0:block] = l0

            @pl.when(col == 1)
            def _():
                o_ref[:, 0:block] = l1
    else:
        o_ref[...] = jnp.zeros_like(o_ref)

    if DO_D and DO_PAN:
        panel_far(lambda c: c.wait_send())
        panel_near(lambda c: c.wait_send(), 0)
        panel_near(lambda c: c.wait_send(), far)
        core_copy(0).wait_send()
    if DO_D:

        @pl.when(is_root)
        def _():
            for k in order:
                scatter_main(k).wait_send()

        gather_sent(d_stream)
    for s in range(SUB):
        for t in range(half):
            plus(t, s).wait_send()
            if t < half - 1:
                minus(t, s).wait_send()
        swap(s).wait_send()
    ext(lambda c: c.wait_send())
    if DO_T:
        gather_sent(t_stream)


def body(matrix, pivots, lower_inverse, upper_inverse):
    local_rows, local_cols = matrix.shape
    block = lower_inverse.shape[1]
    rows_n = lax.axis_size("row")
    cols_n = lax.axis_size("col")
    zn = rows_n // 2
    half = zn // 2
    per = block // zn
    width = local_cols // SUB
    sem = pltpu.SemaphoreType.DMA
    vmem = pltpu.VMEM
    tn = SUB + 1
    return pl.pallas_call(
        functools.partial(kernel, rows_n, cols_n),
        out_shape=jax.ShapeDtypeStruct((local_rows, local_cols), BF16),
        in_specs=[pl.BlockSpec(memory_space=pltpu.VMEM)] * 4,
        out_specs=pl.BlockSpec(memory_space=pltpu.VMEM),
        scratch_shapes=[
            vmem((SUB, zn, 2, per, width), BF16),
            vmem((2, SUB, 2, per, width), BF16),
            vmem((zn, 2, per, block), BF16),
            vmem((half, SUB, 2, per, width), BF16),
            vmem((half - 1, SUB, 2, per, width), BF16),
            vmem((SUB, 2, per, width), BF16),
            vmem((SUB, 2, per, width), BF16),
            vmem((2, SUB, zn, per, width), BF16),
            vmem((2, zn, per, block), BF16),
            vmem((2, zn, per, local_cols), BF16),
            vmem((2, block, block), BF16),
            vmem((block, 2 * block), BF16),
            vmem((block, 128), F32),
            sem((half, SUB)), sem((half, SUB)),
            sem((half - 1, SUB)), sem((half - 1, SUB)),
            sem((SUB,)), sem((SUB,)),
            sem((cols_n,)), sem(()),
            sem((2 * half, tn)), sem((2 * half, tn)),
            sem((2 * half, tn)), sem((2 * half, tn)),
            sem((2 * half, 1)), sem((2 * half, 1)),
            sem((2 * half, 1)), sem((2 * half, 1)),
            sem((cols_n,)), sem((2,)),
            sem((zn,)), sem(()),
        ],
        compiler_params=pltpu.CompilerParams(
            collective_id=0, has_side_effects=True, vmem_limit_bytes=56 << 20
        ),
    )(matrix, pivots, lower_inverse, upper_inverse)


def solution(mesh):
    placed = (P("row", "col"), P(), P(), P())
    return jax.shard_map(
        body, mesh=mesh, in_specs=placed, out_specs=P("row", "col"), check_vma=False
    )
```

```python
import functools

import jax
import jax.numpy as jnp
from jax import lax
from jax.experimental import pallas as pl
from jax.experimental.pallas import tpu as pltpu
from jax.sharding import PartitionSpec as P

MESH = pl.DeviceIdType.MESH
F32 = jnp.float32
BF16 = jnp.bfloat16
SUB = 2
T_HOP = 2
D_HOP = 2
D_START = 2
SC_N = 15
PAN_A = 0
PAN_X = 2
PAN_B = 3


def dot(a, b):
    return jnp.dot(a, b, preferred_element_type=F32)


def kernel(
    rows_n, cols_n,
    a_ref, piv_ref, lo_ref, up_ref, o_ref,
    cand, lead, selh, rp, rm, xr, tb, te, db, pb, gsel, own_ref,
    rp_s, rp_r, rm_s, rm_r, x_s, x_r, e_s, e_r,
    tp_s, tp_r, tx_s, tx_r, dp_s, dp_r, dx_s, dx_r,
    pan_s, pan_r, sc_s, sc_r,
):
    block = lo_ref.shape[1]
    zn = rows_n // 2
    half = zn // 2
    width = cand.shape[-1]
    per = block // zn
    row = lax.axis_index("row")
    col = lax.axis_index("col")
    z = row // 2
    xl = lax.rem(row, 2)
    core = lax.rem(col, 2)
    pair_id = (row + 1 - 2 * xl, col)
    core_id = (row, col + 1 - 2 * core)
    is_root = z == 0
    source = 1 - xl

    def home(k):
        return lax.rem(k + 4 * zn, zn)

    def at_z(i):
        return (2 * home(z + i) + xl, col)

    barrier = pltpu.get_barrier_semaphore()

    def greet(dest):
        pl.semaphore_signal(barrier, inc=1, device_id=dest, device_id_type=MESH)

    reach = max(T_HOP, D_HOP)
    for i in range(1, reach + 1):
        greet(at_z(i))
        greet(at_z(-i))
    greet(pair_id)
    greet(core_id)
    for p in range(2):
        @pl.when(col != p)
        def _():
            greet((row, p))

    @pl.when(col > cols_n // 2 + 1)
    def _():
        greet((row, cols_n // 2 + core))

    @pl.when(z != 0)
    def _():
        greet((xl, col))

    base = (row * block).astype(F32)
    ii = lax.broadcasted_iota(jnp.int32, (block, block), 0).astype(F32)
    jj = lax.broadcasted_iota(jnp.int32, (block, block), 1).astype(F32)
    p0r = piv_ref[0:1, :].astype(F32)
    p1r = piv_ref[1:2, :].astype(F32)
    eye = ii == jj
    p0c = jnp.sum(jnp.where(eye, p0r, 0.0), axis=1, keepdims=True)
    p1c = jnp.sum(jnp.where(eye, p1r, 0.0), axis=1, keepdims=True)
    q1c = p1c + jnp.sum(jnp.where(p1c == p0r, jj - p1c, 0.0), axis=1, keepdims=True)
    selh[:, 0] = jnp.where(p0c == base + jj, 1.0, 0.0).astype(BF16).reshape(zn, per, block)
    selh[:, 1] = jnp.where(q1c == base + jj, 1.0, 0.0).astype(BF16).reshape(zn, per, block)
    firsts = (home(z + half), home(z - half + 1))
    for d in range(2):
        sel = selh[firsts[d]].reshape(2 * per, block)
        for s in range(SUB):
            part = dot(sel, a_ref[:, s * width : (s + 1) * width]).astype(BF16)
            lead[d, :, s] = part.reshape(2, per, width)

    waits = 2 * reach + 2 + jnp.where(col < 2, cols_n - 1, 0) + jnp.where(col // 2 == cols_n // 4, cols_n // 4 - 1, 0) + jnp.where(is_root, zn - 1, 0)
    pl.semaphore_wait(barrier, waits)

    def remote(src, dst, ssem, rsem, dest):
        return pltpu.make_async_remote_copy(
            src_ref=src, dst_ref=dst, send_sem=ssem, recv_sem=rsem,
            device_id=dest, device_id_type=MESH,
        )

    def turn_home(i):
        return home(z + half - i // 2) if i % 2 == 0 or i == zn - 1 else home(z - half + 1 + i // 2)

    order_homes = [turn_home(i) for i in range(zn - 1)] + [z]

    def give(i):
        src = lead.at[i, 1 - xl] if i < 2 else cand.at[order_homes[i], 1 - xl]
        return remote(src, xr.at[i], x_s.at[i], x_r.at[i], pair_id)

    def plus(t, s):
        src = lead.at[0, xl, s] if t == 0 else rp.at[t - 1, s]
        return remote(src, rp.at[t, s], rp_s.at[t, s], rp_r.at[t, s], at_z(1))

    def minus(t, s):
        src = lead.at[1, xl, s] if t == 0 else rm.at[t - 1, s]
        return remote(src, rm.at[t, s], rm_s.at[t, s], rm_r.at[t, s], at_z(-1))

    def reduce_step(t):
        if t == 0:
            for d, chain in ((0, plus), (1, minus)):
                give(d).wait_recv()
                lead[d, xl] = lead[d, xl] + xr[d]
                for s in range(SUB):
                    chain(0, s).start()
            return
        give(2 * t).wait_recv()
        if t < half - 1:
            give(2 * t + 1).wait_recv()
        for s in range(SUB):
            plus(t - 1, s).wait_recv()
            rp[t - 1, s] = rp[t - 1, s] + (cand[order_homes[2 * t], xl, s] + xr[2 * t, s])
            plus(t, s).start()
            if t < half - 1:
                i = 2 * t + 1
                minus(t - 1, s).wait_recv()
                rm[t - 1, s] = rm[t - 1, s] + (cand[order_homes[i], xl, s] + xr[i, s])
                minus(t, s).start()

    def candidates():
        for s in range(SUB):
            sel = selh[...].reshape(zn * 2 * per, block)
            part = dot(sel, a_ref[:, s * width : (s + 1) * width]).astype(BF16)
            cand[:, :, s] = part.reshape(zn, 2, per, width)

    def sources():
        h0 = jnp.where(base + ii == p0r, 1.0, 0.0)
        h1 = jnp.where(base + ii == p1r, 1.0, 0.0)
        any0 = jnp.sum(h0, axis=1, keepdims=True)
        any1 = jnp.sum(h1, axis=1, keepdims=True)
        into1 = jnp.where(p0r == block + ii, 1.0, 0.0)
        from0 = jnp.sum(jnp.where(p0c == block + jj, 1.0, 0.0), axis=0, keepdims=True)
        via = dot(h1.astype(BF16), into1.astype(BF16))
        gsel[:, 0:block] = (via + h0 * (1.0 - any1)).astype(BF16)
        gsel[:, block : 2 * block] = (h1 * (1.0 - from0)).astype(BF16)
        own_ref[...] = jnp.broadcast_to((1.0 - any1) * (1.0 - any0), own_ref.shape)

    def panel_copy(p, other):
        return remote(pb.at[p], pb.at[p], pan_s.at[other], pan_r.at[p], (row, other))

    far = cols_n // 2

    def panel_far(action):
        for p in range(2):
            @pl.when(col == p)
            def _():
                action(panel_copy(p, far + p))

    def panel_near(action, first):
        for p in range(2):
            @pl.when(col == first + p)
            def _():
                for other in range(2, far, 2):
                    action(panel_copy(p, first + p + other))

    def core_copy(p):
        return remote(pb.at[p], pb.at[p], pan_s.at[0], pan_r.at[p], core_id)

    def panel_start():
        @pl.when(col == 0)
        def _():
            pb[0] = dot(o_ref[:, 0:block], up_ref[0]).astype(BF16)

        @pl.when(col == 1)
        def _():
            pb[1] = o_ref[:, 0:block]

        panel_far(lambda c: c.start())
        panel_near(lambda c: c.start(), 0)

    def panel_relay():
        for p in range(2):
            @pl.when(col == far + p)
            def _():
                panel_copy(p, far + p).wait_recv()

        panel_near(lambda c: c.start(), far)

    def panel_pass():
        for p in range(2):
            @pl.when(core == p)
            def _():
                @pl.when(lax.rem(col, far) != p)
                def _():
                    core_copy(p).wait_recv()

                core_copy(p).start()

    def panel_wait():
        for p in range(2):
            @pl.when(core != p)
            def _():
                core_copy(p).wait_recv()

    order = [k if i == 0 else zn - k for k in range(half, 0, -1) for i in range(2) if k < half or i == 0]

    def scatter_main(k):
        return remote(
            a_ref.at[pl.ds(k * per, per)], db.at[xl, k], sc_s.at[k], sc_r,
            (2 * k + xl, col),
        )

    def scatter_start(t):
        @pl.when(is_root)
        def _():
            for k in order[SC_N * t : SC_N * t + SC_N]:
                scatter_main(k).start()
            if t == 0:
                db[xl, 0] = a_ref[0:per, :]

    def scatter_wait():
        @pl.when(z != 0)
        def _():
            scatter_main(1).wait_recv()

    def t_piece(part, j, k):
        return te.at[part, k] if j == 0 else tb.at[part, j - 1, k]

    def d_piece(part, j, k):
        return db.at[part, k]

    t_stream = (t_piece, SUB + 1, T_HOP, tp_s, tp_r, tx_s, tx_r)
    d_stream = (d_piece, 1, D_HOP, dp_s, dp_r, dx_s, dx_r)

    def along(stream, d, m, j, sender):
        piece, _, hop, ssem, rsem, _, _ = stream
        i = (m - 1) % hop + 1
        back = m - i if sender else m
        sign = 1 if d == 0 else -1
        ref = piece(xl, j, home(z - sign * back))
        slot = m if d == 0 else half + m
        return remote(ref, ref, ssem.at[slot, j], rsem.at[slot, j], at_z(sign * i))

    def across(stream, d, m, j):
        piece, _, _, _, _, ssem, rsem = stream
        ref = piece(xl, j, home(z - m if d == 0 else z + m))
        slot = m if d == 0 else half + m
        return remote(ref, ref, ssem.at[slot, j], rsem.at[slot, j], pair_id)

    def across_other(stream, d, m, j):
        piece, _, _, _, _, ssem, rsem = stream
        ref = piece(1 - xl, j, home(z - m if d == 0 else z + m))
        slot = m if d == 0 else half + m
        return remote(ref, ref, ssem.at[slot, j], rsem.at[slot, j], pair_id)

    last = (half, half - 1)

    def send_from(stream, d, u, j):
        hop = stream[2]
        for m in range(hop * u + 1, min(hop * u + hop, last[d]) + 1):
            along(stream, d, m, j, True).start()

    def gather_step(stream, u, js):
        hop = stream[2]
        for j in js:
            if u == 0:
                for d in range(2):
                    send_from(stream, d, 0, j)
                across(stream, 0, 0, j).start()
        if u == 0:
            return
        for i in range(hop, 0, -1):
            m = hop * (u - 1) + i
            for j in js:
                for d in range(2):
                    if m <= last[d]:
                        along(stream, d, m, j, False).wait_recv()
                        if i == hop:
                            send_from(stream, d, u, j)
            for j in js:
                for d in range(2):
                    if m <= last[d]:
                        across(stream, d, m, j).start()

    def steps(stream):
        return -(-half // stream[2]) + 1

    def slots():
        yield 0, 0
        for d in range(2):
            for m in range(1, last[d] + 1):
                yield d, m

    def cross_wait(stream):
        for j in range(stream[1]):
            for d, m in slots():
                across_other(stream, d, m, j).wait_recv()

    def gather_sent(stream):
        for j in range(stream[1]):
            for d, m in slots():
                across(stream, d, m, j).wait_send()
                if m:
                    along(stream, d, m, j, True).wait_send()

    def own_rows(s):
        i = zn - 1
        plus(half - 1, s).wait_recv()
        minus(half - 2, s).wait_recv()
        mine = cand[z, xl, s] + xr[i, s]
        tb[xl, s, z] = mine + rp[half - 1, s] + rm[half - 2, s]

    def ext_copy(other):
        return remote(
            tb.at[xl, 0, z, :, pl.ds(0, block)], te.at[xl, z], e_s.at[other], e_r, (row, other)
        )

    def ext(action):
        for p in range(2):
            @pl.when(jnp.logical_and(col == p, source == p))
            def _():
                for other in range(cols_n):
                    if other != p:
                        action(ext_copy(other))

    def ext_start():
        ext(lambda c: c.start())

        @pl.when(col == source)
        def _():
            te[xl, z] = tb[xl, 0, z, :, 0:block]

    def ext_wait():
        @pl.when(col != source)
        def _():
            ext_copy(0).wait_recv()

    def cols(s):
        return slice(s * width, (s + 1) * width)

    def exchanged():
        own = own_ref[:, 0:1]
        g = gsel[...]
        for s in range(SUB):
            d0 = db[0, :, :, cols(s)].reshape(block, width)
            d1 = db[1, :, :, cols(s)].reshape(block, width)
            x = dot(g, jnp.concatenate([d0, d1], axis=0)) + own * a_ref[:, cols(s)].astype(F32)
            o_ref[:, cols(s)] = x.astype(BF16)

    d_next = [0]

    def d_step():
        if d_next[0] < steps(d_stream):
            if d_next[0] == 0:
                scatter_wait()
            gather_step(d_stream, d_next[0], (0,))
            d_next[0] += 1

    def panel_point(u):
        if u == PAN_A:
            while d_next[0] < steps(d_stream):
                d_step()
            cross_wait(d_stream)
            exchanged()
            panel_start()
        if u == PAN_X:
            panel_relay()
        if u == PAN_B:
            panel_pass()

    give(0).start()
    give(1).start()
    scatter_start(0)
    candidates()
    for i in range(2, zn):
        give(i).start()
    reduce_step(0)
    sources()
    for t in range(1, half):
        reduce_step(t)
        if SC_N < 15:
            scatter_start(t)
        if t >= D_START:
            d_step()
    give(zn - 1).wait_recv()
    for s in range(SUB):
        own_rows(s)
        if s == 0:
            ext_start()
    main = tuple(range(1, SUB + 1))
    gather_step(t_stream, 0, main)
    panel_point(0)
    ext_wait()
    gather_step(t_stream, 0, (0,))
    for u in range(1, steps(t_stream)):
        gather_step(t_stream, u, main + (0,))
        panel_point(u)
    cross_wait(t_stream)
    panel_wait()

    lo0, lo1, up0, up1 = lo_ref[0], lo_ref[1], up_ref[0], up_ref[1]

    ext0 = te[0].reshape(block, block)
    ext1 = te[1].reshape(block, block)
    lower_t = dot(ext1, up0).astype(BF16)

    def top(s):
        t0 = tb[0, s].reshape(block, width)
        t1 = tb[1, s].reshape(block, width)
        return t0, t1, dot(lo0, t0).astype(BF16)

    def second(t1, u0):
        t1u = (t1.astype(F32) - dot(lower_t, u0)).astype(BF16)
        return t1u, dot(lo1, t1u).astype(BF16)

    @pl.when(row == 0)
    def _():
        for s in range(SUB):
            o_ref[:, cols(s)] = top(s)[2]

        @pl.when(col == 0)
        def _():
            o_ref[:, 0:block] = tb[0, 0].reshape(block, width)[:, 0:block]

    @pl.when(row == 1)
    def _():
        for s in range(SUB):
            _, t1, u0 = top(s)
            t1u, u1 = second(t1, u0)
            o_ref[:, cols(s)] = u1
            if s == 0:
                @pl.when(col == 1)
                def _():
                    o_ref[:, 0:block] = t1u[:, 0:block]

        @pl.when(col == 0)
        def _():
            o_ref[:, 0:block] = lower_t

    @pl.when(row > 1)
    def _():
        l0 = pb[0]
        u0e = dot(lo0, ext0).astype(BF16)
        y1 = (pb[1].astype(F32) - dot(l0, u0e)).astype(BF16)
        l1 = dot(y1, up1).astype(BF16)
        ll = jnp.concatenate([l0, l1], axis=1)
        for s in range(SUB):
            _, t1, u0 = top(s)
            _, u1 = second(t1, u0)
            uu = jnp.concatenate([u0, u1], axis=0)
            o_ref[:, cols(s)] = (o_ref[:, cols(s)].astype(F32) - dot(ll, uu)).astype(BF16)

        @pl.when(col == 0)
        def _():
            o_ref[:, 0:block] = l0

        @pl.when(col == 1)
        def _():
            o_ref[:, 0:block] = l1

    panel_far(lambda c: c.wait_send())
    panel_near(lambda c: c.wait_send(), 0)
    panel_near(lambda c: c.wait_send(), far)
    core_copy(0).wait_send()

    @pl.when(is_root)
    def _():
        for k in order:
            scatter_main(k).wait_send()

    gather_sent(d_stream)
    for i in range(zn):
        give(i).wait_send()
    for s in range(SUB):
        for t in range(half):
            plus(t, s).wait_send()
            if t < half - 1:
                minus(t, s).wait_send()
    ext(lambda c: c.wait_send())
    gather_sent(t_stream)


def body(matrix, pivots, lower_inverse, upper_inverse):
    local_rows, local_cols = matrix.shape
    block = lower_inverse.shape[1]
    rows_n = lax.axis_size("row")
    cols_n = lax.axis_size("col")
    zn = rows_n // 2
    half = zn // 2
    per = block // zn
    width = local_cols // SUB
    sem = pltpu.SemaphoreType.DMA
    vmem = pltpu.VMEM
    tn = SUB + 1
    return pl.pallas_call(
        functools.partial(kernel, rows_n, cols_n),
        out_shape=jax.ShapeDtypeStruct((local_rows, local_cols), BF16),
        in_specs=[pl.BlockSpec(memory_space=pltpu.VMEM)] * 4,
        out_specs=pl.BlockSpec(memory_space=pltpu.VMEM),
        scratch_shapes=[
            vmem((zn, 2, SUB, per, width), BF16),
            vmem((2, 2, SUB, per, width), BF16),
            vmem((zn, 2, per, block), BF16),
            vmem((half, SUB, per, width), BF16),
            vmem((half - 1, SUB, per, width), BF16),
            vmem((zn, SUB, per, width), BF16),
            vmem((2, SUB, zn, per, width), BF16),
            vmem((2, zn, per, block), BF16),
            vmem((2, zn, per, local_cols), BF16),
            vmem((2, block, block), BF16),
            vmem((block, 2 * block), BF16),
            vmem((block, 128), F32),
            sem((half, SUB)), sem((half, SUB)),
            sem((half - 1, SUB)), sem((half - 1, SUB)),
            sem((zn,)), sem((zn,)),
            sem((cols_n,)), sem(()),
            sem((2 * half, tn)), sem((2 * half, tn)),
            sem((2 * half, tn)), sem((2 * half, tn)),
            sem((2 * half, 1)), sem((2 * half, 1)),
            sem((2 * half, 1)), sem((2 * half, 1)),
            sem((cols_n,)), sem((2,)),
            sem((zn,)), sem(()),
        ],
        compiler_params=pltpu.CompilerParams(
            collective_id=0, has_side_effects=True, vmem_limit_bytes=56 << 20
        ),
    )(matrix, pivots, lower_inverse, upper_inverse)


def solution(mesh):
    placed = (P("row", "col"), P(), P(), P())
    return jax.shard_map(
        body, mesh=mesh, in_specs=placed, out_specs=P("row", "col"), check_vma=False
    )
```

```python
import functools

import jax
import jax.numpy as jnp
from jax import lax
from jax.experimental import pallas as pl
from jax.experimental.pallas import tpu as pltpu
from jax.sharding import PartitionSpec as P

MESH = pl.DeviceIdType.MESH
F32 = jnp.float32
BF16 = jnp.bfloat16
SUB = 2
T_HOP = 2
D_HOP = 2
D_START = 2
SC_N = 15
PAN_A = 0
PAN_X = 2
PAN_B = 3
VLIM = 24
D_MORE = 0


def dot(a, b):
    return jnp.dot(a, b, preferred_element_type=F32)


def kernel(
    rows_n, cols_n,
    a_hbm, piv_hbm, lo_hbm, up_hbm, o_ref,
    piv_ref, a_ref, lo_ref, up_ref, load_sem,
    cand, lead, selh, rp, rm, xr, tb, te, db, pb, gsel, own_ref,
    rp_s, rp_r, rm_s, rm_r, x_s, x_r, e_s, e_r,
    tp_s, tp_r, tx_s, tx_r, dp_s, dp_r, dx_s, dx_r,
    pan_s, pan_r, sc_s, sc_r,
):
    block = lo_hbm.shape[1]
    zn = rows_n // 2
    half = zn // 2
    width = cand.shape[-1]
    per = block // zn
    row = lax.axis_index("row")
    col = lax.axis_index("col")
    z = row // 2
    xl = lax.rem(row, 2)
    core = lax.rem(col, 2)
    pair_id = (row + 1 - 2 * xl, col)
    core_id = (row, col + 1 - 2 * core)
    is_root = z == 0
    source = 1 - xl

    def home(k):
        return lax.rem(k + 4 * zn, zn)

    def at_z(i):
        return (2 * home(z + i) + xl, col)

    barrier = pltpu.get_barrier_semaphore()

    def greet(dest):
        pl.semaphore_signal(barrier, inc=1, device_id=dest, device_id_type=MESH)

    reach = max(T_HOP, D_HOP)
    for i in range(1, reach + 1):
        greet(at_z(i))
        greet(at_z(-i))
    greet(pair_id)
    greet(core_id)
    for p in range(2):
        @pl.when(col != p)
        def _():
            greet((row, p))

    @pl.when(col > cols_n // 2 + 1)
    def _():
        greet((row, cols_n // 2 + core))

    @pl.when(z != 0)
    def _():
        greet((xl, col))

    loads = [
        pltpu.make_async_copy(src, dst, load_sem.at[i])
        for i, (src, dst) in enumerate(((piv_hbm, piv_ref), (a_hbm, a_ref), (lo_hbm, lo_ref), (up_hbm, up_ref)))
    ]
    for load in loads:
        load.start()
    loads[0].wait()

    base = (row * block).astype(F32)
    ii = lax.broadcasted_iota(jnp.int32, (block, block), 0).astype(F32)
    jj = lax.broadcasted_iota(jnp.int32, (block, block), 1).astype(F32)
    p0r = piv_ref[0:1, :].astype(F32)
    p1r = piv_ref[1:2, :].astype(F32)
    eye = ii == jj
    p0c = jnp.sum(jnp.where(eye, p0r, 0.0), axis=1, keepdims=True)
    p1c = jnp.sum(jnp.where(eye, p1r, 0.0), axis=1, keepdims=True)
    q1c = p1c + jnp.sum(jnp.where(p1c == p0r, jj - p1c, 0.0), axis=1, keepdims=True)
    selh[:, 0] = jnp.where(p0c == base + jj, 1.0, 0.0).astype(BF16).reshape(zn, per, block)
    selh[:, 1] = jnp.where(q1c == base + jj, 1.0, 0.0).astype(BF16).reshape(zn, per, block)
    loads[1].wait()
    firsts = (home(z + half), home(z - half + 1))
    for d in range(2):
        sel = selh[firsts[d]].reshape(2 * per, block)
        for s in range(SUB):
            part = dot(sel, a_ref[:, s * width : (s + 1) * width]).astype(BF16)
            lead[d, :, s] = part.reshape(2, per, width)

    waits = 2 * reach + 2 + jnp.where(col < 2, cols_n - 1, 0) + jnp.where(col // 2 == cols_n // 4, cols_n // 4 - 1, 0) + jnp.where(is_root, zn - 1, 0)
    pl.semaphore_wait(barrier, waits)

    def remote(src, dst, ssem, rsem, dest):
        return pltpu.make_async_remote_copy(
            src_ref=src, dst_ref=dst, send_sem=ssem, recv_sem=rsem,
            device_id=dest, device_id_type=MESH,
        )

    def turn_home(i):
        return home(z + half - i // 2) if i % 2 == 0 or i == zn - 1 else home(z - half + 1 + i // 2)

    order_homes = [turn_home(i) for i in range(zn - 1)] + [z]

    def give(i):
        src = lead.at[i, 1 - xl] if i < 2 else cand.at[order_homes[i], 1 - xl]
        return remote(src, xr.at[i], x_s.at[i], x_r.at[i], pair_id)

    def plus(t, s):
        src = lead.at[0, xl, s] if t == 0 else rp.at[t - 1, s]
        return remote(src, rp.at[t, s], rp_s.at[t, s], rp_r.at[t, s], at_z(1))

    def minus(t, s):
        src = lead.at[1, xl, s] if t == 0 else rm.at[t - 1, s]
        return remote(src, rm.at[t, s], rm_s.at[t, s], rm_r.at[t, s], at_z(-1))

    def reduce_step(t):
        if t == 0:
            for d, chain in ((0, plus), (1, minus)):
                give(d).wait_recv()
                lead[d, xl] = lead[d, xl] + xr[d]
                for s in range(SUB):
                    chain(0, s).start()
            return
        give(2 * t).wait_recv()
        if t < half - 1:
            give(2 * t + 1).wait_recv()
        for s in range(SUB):
            plus(t - 1, s).wait_recv()
            rp[t - 1, s] = rp[t - 1, s] + (cand[order_homes[2 * t], xl, s] + xr[2 * t, s])
            plus(t, s).start()
            if t < half - 1:
                i = 2 * t + 1
                minus(t - 1, s).wait_recv()
                rm[t - 1, s] = rm[t - 1, s] + (cand[order_homes[i], xl, s] + xr[i, s])
                minus(t, s).start()

    def candidates():
        for s in range(SUB):
            sel = selh[...].reshape(zn * 2 * per, block)
            part = dot(sel, a_ref[:, s * width : (s + 1) * width]).astype(BF16)
            cand[:, :, s] = part.reshape(zn, 2, per, width)

    def sources():
        h0 = jnp.where(base + ii == p0r, 1.0, 0.0)
        h1 = jnp.where(base + ii == p1r, 1.0, 0.0)
        any0 = jnp.sum(h0, axis=1, keepdims=True)
        any1 = jnp.sum(h1, axis=1, keepdims=True)
        into1 = jnp.where(p0r == block + ii, 1.0, 0.0)
        from0 = jnp.sum(jnp.where(p0c == block + jj, 1.0, 0.0), axis=0, keepdims=True)
        via = dot(h1.astype(BF16), into1.astype(BF16))
        gsel[:, 0:block] = (via + h0 * (1.0 - any1)).astype(BF16)
        gsel[:, block : 2 * block] = (h1 * (1.0 - from0)).astype(BF16)
        own_ref[...] = jnp.broadcast_to((1.0 - any1) * (1.0 - any0), own_ref.shape)

    def panel_copy(p, other):
        return remote(pb.at[p], pb.at[p], pan_s.at[other], pan_r.at[p], (row, other))

    far = cols_n // 2

    def panel_far(action):
        for p in range(2):
            @pl.when(col == p)
            def _():
                action(panel_copy(p, far + p))

    def panel_near(action, first):
        for p in range(2):
            @pl.when(col == first + p)
            def _():
                for other in range(2, far, 2):
                    action(panel_copy(p, first + p + other))

    def core_copy(p):
        return remote(pb.at[p], pb.at[p], pan_s.at[0], pan_r.at[p], core_id)

    def panel_start():
        @pl.when(col == 0)
        def _():
            pb[0] = dot(o_ref[:, 0:block], up_ref[0]).astype(BF16)

        @pl.when(col == 1)
        def _():
            pb[1] = o_ref[:, 0:block]

        panel_far(lambda c: c.start())
        panel_near(lambda c: c.start(), 0)

    def panel_relay():
        for p in range(2):
            @pl.when(col == far + p)
            def _():
                panel_copy(p, far + p).wait_recv()

        panel_near(lambda c: c.start(), far)

    def panel_pass():
        for p in range(2):
            @pl.when(core == p)
            def _():
                @pl.when(lax.rem(col, far) != p)
                def _():
                    core_copy(p).wait_recv()

                core_copy(p).start()

    def panel_wait():
        for p in range(2):
            @pl.when(core != p)
            def _():
                core_copy(p).wait_recv()

    order = [k if i == 0 else zn - k for k in range(half, 0, -1) for i in range(2) if k < half or i == 0]

    def scatter_main(k):
        return remote(
            a_ref.at[pl.ds(k * per, per)], db.at[xl, k], sc_s.at[k], sc_r,
            (2 * k + xl, col),
        )

    def scatter_start(t):
        @pl.when(is_root)
        def _():
            for k in order[SC_N * t : SC_N * t + SC_N]:
                scatter_main(k).start()
            if t == 0:
                db[xl, 0] = a_ref[0:per, :]

    def scatter_wait():
        @pl.when(z != 0)
        def _():
            scatter_main(1).wait_recv()

    def t_piece(part, j, k):
        return te.at[part, k] if j == 0 else tb.at[part, j - 1, k]

    def d_piece(part, j, k):
        return db.at[part, k]

    t_stream = (t_piece, SUB + 1, T_HOP, tp_s, tp_r, tx_s, tx_r)
    d_stream = (d_piece, 1, D_HOP, dp_s, dp_r, dx_s, dx_r)

    def along(stream, d, m, j, sender):
        piece, _, hop, ssem, rsem, _, _ = stream
        i = (m - 1) % hop + 1
        back = m - i if sender else m
        sign = 1 if d == 0 else -1
        ref = piece(xl, j, home(z - sign * back))
        slot = m if d == 0 else half + m
        return remote(ref, ref, ssem.at[slot, j], rsem.at[slot, j], at_z(sign * i))

    def across(stream, d, m, j):
        piece, _, _, _, _, ssem, rsem = stream
        ref = piece(xl, j, home(z - m if d == 0 else z + m))
        slot = m if d == 0 else half + m
        return remote(ref, ref, ssem.at[slot, j], rsem.at[slot, j], pair_id)

    def across_other(stream, d, m, j):
        piece, _, _, _, _, ssem, rsem = stream
        ref = piece(1 - xl, j, home(z - m if d == 0 else z + m))
        slot = m if d == 0 else half + m
        return remote(ref, ref, ssem.at[slot, j], rsem.at[slot, j], pair_id)

    last = (half, half - 1)

    def send_from(stream, d, u, j):
        hop = stream[2]
        for m in range(hop * u + 1, min(hop * u + hop, last[d]) + 1):
            along(stream, d, m, j, True).start()

    def gather_step(stream, u, js):
        hop = stream[2]
        for j in js:
            if u == 0:
                for d in range(2):
                    send_from(stream, d, 0, j)
                across(stream, 0, 0, j).start()
        if u == 0:
            return
        for i in range(hop, 0, -1):
            m = hop * (u - 1) + i
            for j in js:
                for d in range(2):
                    if m <= last[d]:
                        along(stream, d, m, j, False).wait_recv()
                        if i == hop:
                            send_from(stream, d, u, j)
            for j in js:
                for d in range(2):
                    if m <= last[d]:
                        across(stream, d, m, j).start()

    def steps(stream):
        return -(-half // stream[2]) + 1

    def slots():
        yield 0, 0
        for d in range(2):
            for m in range(1, last[d] + 1):
                yield d, m

    def cross_wait(stream, j):
        for d, m in slots():
            across_other(stream, d, m, j).wait_recv()

    def gather_sent(stream):
        for j in range(stream[1]):
            for d, m in slots():
                across(stream, d, m, j).wait_send()
                if m:
                    along(stream, d, m, j, True).wait_send()

    def own_rows(s):
        i = zn - 1
        plus(half - 1, s).wait_recv()
        minus(half - 2, s).wait_recv()
        mine = cand[z, xl, s] + xr[i, s]
        tb[xl, s, z] = mine + rp[half - 1, s] + rm[half - 2, s]

    def ext_copy(other):
        return remote(
            tb.at[xl, 0, z, :, pl.ds(0, block)], te.at[xl, z], e_s.at[other], e_r, (row, other)
        )

    def ext(action):
        for p in range(2):
            @pl.when(jnp.logical_and(col == p, source == p))
            def _():
                for other in range(cols_n):
                    if other != p:
                        action(ext_copy(other))

    def ext_start():
        ext(lambda c: c.start())

        @pl.when(col == source)
        def _():
            te[xl, z] = tb[xl, 0, z, :, 0:block]

    def ext_wait():
        @pl.when(col != source)
        def _():
            ext_copy(0).wait_recv()

    def cols(s):
        return slice(s * width, (s + 1) * width)

    def exchanged():
        own = own_ref[:, 0:1]
        g = gsel[...]
        for s in range(SUB):
            d0 = db[0, :, :, cols(s)].reshape(block, width)
            d1 = db[1, :, :, cols(s)].reshape(block, width)
            x = dot(g, jnp.concatenate([d0, d1], axis=0)) + own * a_ref[:, cols(s)].astype(F32)
            o_ref[:, cols(s)] = x.astype(BF16)

    d_next = [0]

    def d_step():
        if d_next[0] < steps(d_stream):
            if d_next[0] == 0:
                scatter_wait()
            gather_step(d_stream, d_next[0], (0,))
            d_next[0] += 1

    def panel_point(u):
        if u == PAN_A:
            while d_next[0] < steps(d_stream):
                d_step()
            cross_wait(d_stream, 0)
            exchanged()
            panel_start()
        if u == PAN_X:
            panel_relay()
        if u == PAN_B:
            panel_pass()

    give(0).start()
    give(1).start()
    scatter_start(0)
    candidates()
    loads[2].wait()
    loads[3].wait()
    for i in range(2, zn):
        give(i).start()
    reduce_step(0)
    sources()
    for t in range(1, half):
        reduce_step(t)
        if SC_N < 15:
            scatter_start(t)
        if t >= D_START:
            d_step()
    give(zn - 1).wait_recv()
    for s in range(SUB):
        own_rows(s)
        if s == 0:
            ext_start()
    if D_MORE > 0:
        d_step()
    main = tuple(range(1, SUB + 1))
    gather_step(t_stream, 0, main)
    if D_MORE > 1:
        d_step()
    panel_point(0)
    ext_wait()
    gather_step(t_stream, 0, (0,))
    for u in range(1, steps(t_stream)):
        gather_step(t_stream, u, main + (0,))
        if D_MORE > 2:
            d_step()
        panel_point(u)
    cross_wait(t_stream, 0)
    panel_wait()

    lo0, lo1, up0, up1 = lo_ref[0], lo_ref[1], up_ref[0], up_ref[1]

    ext0 = te[0].reshape(block, block)
    ext1 = te[1].reshape(block, block)
    lower_t = dot(ext1, up0).astype(BF16)

    def top(s):
        cross_wait(t_stream, s + 1)
        t0 = tb[0, s].reshape(block, width)
        t1 = tb[1, s].reshape(block, width)
        return t0, t1, dot(lo0, t0).astype(BF16)

    def second(t1, u0):
        t1u = (t1.astype(F32) - dot(lower_t, u0)).astype(BF16)
        return t1u, dot(lo1, t1u).astype(BF16)

    @pl.when(row == 0)
    def _():
        for s in range(SUB):
            o_ref[:, cols(s)] = top(s)[2]

        @pl.when(col == 0)
        def _():
            o_ref[:, 0:block] = tb[0, 0].reshape(block, width)[:, 0:block]

    @pl.when(row == 1)
    def _():
        for s in range(SUB):
            _, t1, u0 = top(s)
            t1u, u1 = second(t1, u0)
            o_ref[:, cols(s)] = u1
            if s == 0:
                @pl.when(col == 1)
                def _():
                    o_ref[:, 0:block] = t1u[:, 0:block]

        @pl.when(col == 0)
        def _():
            o_ref[:, 0:block] = lower_t

    @pl.when(row > 1)
    def _():
        l0 = pb[0]
        u0e = dot(lo0, ext0).astype(BF16)
        y1 = (pb[1].astype(F32) - dot(l0, u0e)).astype(BF16)
        l1 = dot(y1, up1).astype(BF16)
        ll = jnp.concatenate([l0, l1], axis=1)
        for s in range(SUB):
            _, t1, u0 = top(s)
            _, u1 = second(t1, u0)
            uu = jnp.concatenate([u0, u1], axis=0)
            o_ref[:, cols(s)] = (o_ref[:, cols(s)].astype(F32) - dot(ll, uu)).astype(BF16)

        @pl.when(col == 0)
        def _():
            o_ref[:, 0:block] = l0

        @pl.when(col == 1)
        def _():
            o_ref[:, 0:block] = l1

    panel_far(lambda c: c.wait_send())
    panel_near(lambda c: c.wait_send(), 0)
    panel_near(lambda c: c.wait_send(), far)
    core_copy(0).wait_send()

    @pl.when(is_root)
    def _():
        for k in order:
            scatter_main(k).wait_send()

    gather_sent(d_stream)
    for i in range(zn):
        give(i).wait_send()
    for s in range(SUB):
        for t in range(half):
            plus(t, s).wait_send()
            if t < half - 1:
                minus(t, s).wait_send()
    ext(lambda c: c.wait_send())
    gather_sent(t_stream)


def pin(x):
    return pltpu.with_memory_space_constraint(x, pltpu.MemorySpace.HBM)


def body(matrix, pivots, lower_inverse, upper_inverse):
    local_rows, local_cols = matrix.shape
    block = lower_inverse.shape[1]
    rows_n = lax.axis_size("row")
    cols_n = lax.axis_size("col")
    zn = rows_n // 2
    half = zn // 2
    per = block // zn
    width = local_cols // SUB
    sem = pltpu.SemaphoreType.DMA
    vmem = pltpu.VMEM
    tn = SUB + 1
    return pl.pallas_call(
        functools.partial(kernel, rows_n, cols_n),
        out_shape=jax.ShapeDtypeStruct((local_rows, local_cols), BF16),
        in_specs=[
            pl.BlockSpec(memory_space=pltpu.MemorySpace.HBM),
            pl.BlockSpec(memory_space=pltpu.MemorySpace.HBM),
            pl.BlockSpec(memory_space=pltpu.MemorySpace.HBM),
            pl.BlockSpec(memory_space=pltpu.MemorySpace.HBM),
        ],
        out_specs=pl.BlockSpec(memory_space=pltpu.VMEM),
        scratch_shapes=[
            vmem(pivots.shape, jnp.int32),
            vmem((local_rows, local_cols), BF16),
            vmem(lower_inverse.shape, BF16),
            vmem(upper_inverse.shape, BF16),
            sem((4,)),
            vmem((zn, 2, SUB, per, width), BF16),
            vmem((2, 2, SUB, per, width), BF16),
            vmem((zn, 2, per, block), BF16),
            vmem((half, SUB, per, width), BF16),
            vmem((half - 1, SUB, per, width), BF16),
            vmem((zn, SUB, per, width), BF16),
            vmem((2, SUB, zn, per, width), BF16),
            vmem((2, zn, per, block), BF16),
            vmem((2, zn, per, local_cols), BF16),
            vmem((2, block, block), BF16),
            vmem((block, 2 * block), BF16),
            vmem((block, 128), F32),
            sem((half, SUB)), sem((half, SUB)),
            sem((half - 1, SUB)), sem((half - 1, SUB)),
            sem((zn,)), sem((zn,)),
            sem((cols_n,)), sem(()),
            sem((2 * half, tn)), sem((2 * half, tn)),
            sem((2 * half, tn)), sem((2 * half, tn)),
            sem((2 * half, 1)), sem((2 * half, 1)),
            sem((2 * half, 1)), sem((2 * half, 1)),
            sem((cols_n,)), sem((2,)),
            sem((zn,)), sem(()),
        ],
        compiler_params=pltpu.CompilerParams(
            collective_id=0, has_side_effects=True, vmem_limit_bytes=VLIM << 20
        ),
    )(pin(matrix), pin(pivots), pin(lower_inverse), pin(upper_inverse))


def solution(mesh):
    placed = (P("row", "col"), P(), P(), P())
    return jax.shard_map(
        body, mesh=mesh, in_specs=placed, out_specs=P("row", "col"), check_vma=False
    )
```

```python
import functools

import jax
import jax.numpy as jnp
from jax import lax
from jax.experimental import pallas as pl
from jax.experimental.pallas import tpu as pltpu
from jax.sharding import PartitionSpec as P

MESH = pl.DeviceIdType.MESH
F32 = jnp.float32
BF16 = jnp.bfloat16
SUB = 2
T_HOP = 2
D_HOP = 2
D_START = 2
SC_N = 15
PAN_A = 0
PAN_X = 1
PAN_B = 2
VLIM = 24
D_MORE = 0


def dot(a, b):
    return jnp.dot(a, b, preferred_element_type=F32)


def kernel(
    rows_n, cols_n,
    a_hbm, piv_hbm, lo_hbm, up_hbm, o_ref,
    piv_ref, a_ref, lo_ref, up_ref, load_sem,
    cand, lead, selh, rp, rm, xr, tb, te, db, pb, gsel, own_ref,
    rp_s, rp_r, rm_s, rm_r, x_s, x_r, e_s, e_r,
    tp_s, tp_r, tx_s, tx_r, dp_s, dp_r, dx_s, dx_r,
    pan_s, pan_r, sc_s, sc_r,
):
    block = lo_hbm.shape[1]
    zn = rows_n // 2
    half = zn // 2
    width = cand.shape[-1]
    per = block // zn
    row = lax.axis_index("row")
    col = lax.axis_index("col")
    z = row // 2
    xl = lax.rem(row, 2)
    core = lax.rem(col, 2)
    pair_id = (row + 1 - 2 * xl, col)
    core_id = (row, col + 1 - 2 * core)
    is_root = z == 0
    source = 1 - xl

    def home(k):
        return lax.rem(k + 4 * zn, zn)

    def at_z(i):
        return (2 * home(z + i) + xl, col)

    barrier = pltpu.get_barrier_semaphore()

    def greet(dest):
        pl.semaphore_signal(barrier, inc=1, device_id=dest, device_id_type=MESH)

    reach = max(T_HOP, D_HOP)
    for i in range(1, reach + 1):
        greet(at_z(i))
        greet(at_z(-i))
    greet(pair_id)
    greet(core_id)
    for p in range(2):
        @pl.when(col != p)
        def _():
            greet((row, p))

    @pl.when(col > cols_n // 2 + 1)
    def _():
        greet((row, cols_n // 2 + core))

    @pl.when(z != 0)
    def _():
        greet((xl, col))

    loads = [
        pltpu.make_async_copy(src, dst, load_sem.at[i])
        for i, (src, dst) in enumerate(((piv_hbm, piv_ref), (a_hbm, a_ref), (lo_hbm, lo_ref), (up_hbm, up_ref)))
    ]
    for load in loads:
        load.start()
    loads[0].wait()

    base = (row * block).astype(F32)
    ii = lax.broadcasted_iota(jnp.int32, (block, block), 0).astype(F32)
    jj = lax.broadcasted_iota(jnp.int32, (block, block), 1).astype(F32)
    p0r = piv_ref[0:1, :].astype(F32)
    p1r = piv_ref[1:2, :].astype(F32)
    eye = ii == jj
    p0c = jnp.sum(jnp.where(eye, p0r, 0.0), axis=1, keepdims=True)
    p1c = jnp.sum(jnp.where(eye, p1r, 0.0), axis=1, keepdims=True)
    q1c = p1c + jnp.sum(jnp.where(p1c == p0r, jj - p1c, 0.0), axis=1, keepdims=True)
    selh[:, 0] = jnp.where(p0c == base + jj, 1.0, 0.0).astype(BF16).reshape(zn, per, block)
    selh[:, 1] = jnp.where(q1c == base + jj, 1.0, 0.0).astype(BF16).reshape(zn, per, block)
    loads[1].wait()
    firsts = (home(z + half), home(z - half + 1))
    for d in range(2):
        sel = selh[firsts[d]].reshape(2 * per, block)
        for s in range(SUB):
            part = dot(sel, a_ref[:, s * width : (s + 1) * width]).astype(BF16)
            lead[d, :, s] = part.reshape(2, per, width)

    waits = 2 * reach + 2 + jnp.where(col < 2, cols_n - 1, 0) + jnp.where(col // 2 == cols_n // 4, cols_n // 4 - 1, 0) + jnp.where(is_root, zn - 1, 0)
    pl.semaphore_wait(barrier, waits)

    def remote(src, dst, ssem, rsem, dest):
        return pltpu.make_async_remote_copy(
            src_ref=src, dst_ref=dst, send_sem=ssem, recv_sem=rsem,
            device_id=dest, device_id_type=MESH,
        )

    def turn_home(i):
        return home(z + half - i // 2) if i % 2 == 0 or i == zn - 1 else home(z - half + 1 + i // 2)

    order_homes = [turn_home(i) for i in range(zn - 1)] + [z]

    def give(i):
        src = lead.at[i, 1 - xl] if i < 2 else cand.at[order_homes[i], 1 - xl]
        return remote(src, xr.at[i], x_s.at[i], x_r.at[i], pair_id)

    def plus(t, s):
        src = lead.at[0, xl, s] if t == 0 else rp.at[t - 1, s]
        return remote(src, rp.at[t, s], rp_s.at[t, s], rp_r.at[t, s], at_z(1))

    def minus(t, s):
        src = lead.at[1, xl, s] if t == 0 else rm.at[t - 1, s]
        return remote(src, rm.at[t, s], rm_s.at[t, s], rm_r.at[t, s], at_z(-1))

    def reduce_step(t):
        if t == 0:
            for d, chain in ((0, plus), (1, minus)):
                give(d).wait_recv()
                lead[d, xl] = lead[d, xl] + xr[d]
                for s in range(SUB):
                    chain(0, s).start()
            return
        give(2 * t).wait_recv()
        if t < half - 1:
            give(2 * t + 1).wait_recv()
        for s in range(SUB):
            plus(t - 1, s).wait_recv()
            rp[t - 1, s] = rp[t - 1, s] + (cand[order_homes[2 * t], xl, s] + xr[2 * t, s])
            plus(t, s).start()
            if t < half - 1:
                i = 2 * t + 1
                minus(t - 1, s).wait_recv()
                rm[t - 1, s] = rm[t - 1, s] + (cand[order_homes[i], xl, s] + xr[i, s])
                minus(t, s).start()

    def candidates():
        for s in range(SUB):
            sel = selh[...].reshape(zn * 2 * per, block)
            part = dot(sel, a_ref[:, s * width : (s + 1) * width]).astype(BF16)
            cand[:, :, s] = part.reshape(zn, 2, per, width)

    def sources():
        h0 = jnp.where(base + ii == p0r, 1.0, 0.0)
        h1 = jnp.where(base + ii == p1r, 1.0, 0.0)
        any0 = jnp.sum(h0, axis=1, keepdims=True)
        any1 = jnp.sum(h1, axis=1, keepdims=True)
        into1 = jnp.where(p0r == block + ii, 1.0, 0.0)
        from0 = jnp.sum(jnp.where(p0c == block + jj, 1.0, 0.0), axis=0, keepdims=True)
        via = dot(h1.astype(BF16), into1.astype(BF16))
        gsel[:, 0:block] = (via + h0 * (1.0 - any1)).astype(BF16)
        gsel[:, block : 2 * block] = (h1 * (1.0 - from0)).astype(BF16)
        own_ref[...] = jnp.broadcast_to((1.0 - any1) * (1.0 - any0), own_ref.shape)

    def panel_copy(p, other):
        return remote(pb.at[p], pb.at[p], pan_s.at[other], pan_r.at[p], (row, other))

    far = cols_n // 2

    def panel_far(action):
        for p in range(2):
            @pl.when(col == p)
            def _():
                action(panel_copy(p, far + p))

    def panel_near(action, first):
        for p in range(2):
            @pl.when(col == first + p)
            def _():
                for other in range(2, far, 2):
                    action(panel_copy(p, first + p + other))

    def core_copy(p):
        return remote(pb.at[p], pb.at[p], pan_s.at[0], pan_r.at[p], core_id)

    def panel_start():
        @pl.when(col == 0)
        def _():
            pb[0] = dot(o_ref[:, 0:block], up_ref[0]).astype(BF16)

        @pl.when(col == 1)
        def _():
            pb[1] = o_ref[:, 0:block]

        panel_far(lambda c: c.start())
        panel_near(lambda c: c.start(), 0)

    def panel_relay():
        for p in range(2):
            @pl.when(col == far + p)
            def _():
                panel_copy(p, far + p).wait_recv()

        panel_near(lambda c: c.start(), far)

    def panel_pass():
        for p in range(2):
            @pl.when(core == p)
            def _():
                @pl.when(lax.rem(col, far) != p)
                def _():
                    core_copy(p).wait_recv()

                core_copy(p).start()

    def panel_wait():
        for p in range(2):
            @pl.when(core != p)
            def _():
                core_copy(p).wait_recv()

    order = [k if i == 0 else zn - k for k in range(half, 0, -1) for i in range(2) if k < half or i == 0]

    def scatter_main(k):
        return remote(
            a_ref.at[pl.ds(k * per, per)], db.at[xl, k], sc_s.at[k], sc_r,
            (2 * k + xl, col),
        )

    def scatter_start(t):
        @pl.when(is_root)
        def _():
            for k in order[SC_N * t : SC_N * t + SC_N]:
                scatter_main(k).start()
            if t == 0:
                db[xl, 0] = a_ref[0:per, :]

    def scatter_wait():
        @pl.when(z != 0)
        def _():
            scatter_main(1).wait_recv()

    def t_piece(part, j, k):
        return te.at[part, k] if j == 0 else tb.at[part, j - 1, k]

    def d_piece(part, j, k):
        return db.at[part, k]

    t_stream = (t_piece, SUB + 1, T_HOP, tp_s, tp_r, tx_s, tx_r)
    d_stream = (d_piece, 1, D_HOP, dp_s, dp_r, dx_s, dx_r)

    def along(stream, d, m, j, sender):
        piece, _, hop, ssem, rsem, _, _ = stream
        i = (m - 1) % hop + 1
        back = m - i if sender else m
        sign = 1 if d == 0 else -1
        ref = piece(xl, j, home(z - sign * back))
        slot = m if d == 0 else half + m
        return remote(ref, ref, ssem.at[slot, j], rsem.at[slot, j], at_z(sign * i))

    def across(stream, d, m, j):
        piece, _, _, _, _, ssem, rsem = stream
        ref = piece(xl, j, home(z - m if d == 0 else z + m))
        slot = m if d == 0 else half + m
        return remote(ref, ref, ssem.at[slot, j], rsem.at[slot, j], pair_id)

    def across_other(stream, d, m, j):
        piece, _, _, _, _, ssem, rsem = stream
        ref = piece(1 - xl, j, home(z - m if d == 0 else z + m))
        slot = m if d == 0 else half + m
        return remote(ref, ref, ssem.at[slot, j], rsem.at[slot, j], pair_id)

    last = (half, half - 1)

    def send_from(stream, d, u, j):
        hop = stream[2]
        for m in range(hop * u + 1, min(hop * u + hop, last[d]) + 1):
            along(stream, d, m, j, True).start()

    def gather_step(stream, u, js):
        hop = stream[2]
        for j in js:
            if u == 0:
                for d in range(2):
                    send_from(stream, d, 0, j)
                across(stream, 0, 0, j).start()
        if u == 0:
            return
        for i in range(hop, 0, -1):
            m = hop * (u - 1) + i
            for j in js:
                for d in range(2):
                    if m <= last[d]:
                        along(stream, d, m, j, False).wait_recv()
                        if i == hop:
                            send_from(stream, d, u, j)
            for j in js:
                for d in range(2):
                    if m <= last[d]:
                        across(stream, d, m, j).start()

    def steps(stream):
        return -(-half // stream[2]) + 1

    def slots():
        yield 0, 0
        for d in range(2):
            for m in range(1, last[d] + 1):
                yield d, m

    def cross_wait(stream, j):
        for d, m in slots():
            across_other(stream, d, m, j).wait_recv()

    def gather_sent(stream):
        for j in range(stream[1]):
            for d, m in slots():
                across(stream, d, m, j).wait_send()
                if m:
                    along(stream, d, m, j, True).wait_send()

    def own_rows(s):
        i = zn - 1
        plus(half - 1, s).wait_recv()
        minus(half - 2, s).wait_recv()
        mine = cand[z, xl, s] + xr[i, s]
        tb[xl, s, z] = mine + rp[half - 1, s] + rm[half - 2, s]

    def ext_copy(other):
        return remote(
            tb.at[xl, 0, z, :, pl.ds(0, block)], te.at[xl, z], e_s.at[other], e_r, (row, other)
        )

    def ext(action):
        for p in range(2):
            @pl.when(jnp.logical_and(col == p, source == p))
            def _():
                for other in range(cols_n):
                    if other != p:
                        action(ext_copy(other))

    def ext_start():
        ext(lambda c: c.start())

        @pl.when(col == source)
        def _():
            te[xl, z] = tb[xl, 0, z, :, 0:block]

    def ext_wait():
        @pl.when(col != source)
        def _():
            ext_copy(0).wait_recv()

    def cols(s):
        return slice(s * width, (s + 1) * width)

    def exchanged():
        own = own_ref[:, 0:1]
        g = gsel[...]
        for s in range(SUB):
            d0 = db[0, :, :, cols(s)].reshape(block, width)
            d1 = db[1, :, :, cols(s)].reshape(block, width)
            x = dot(g, jnp.concatenate([d0, d1], axis=0)) + own * a_ref[:, cols(s)].astype(F32)
            o_ref[:, cols(s)] = x.astype(BF16)

    d_next = [0]

    def d_step():
        if d_next[0] < steps(d_stream):
            if d_next[0] == 0:
                scatter_wait()
            gather_step(d_stream, d_next[0], (0,))
            d_next[0] += 1

    def panel_point(u):
        if u == PAN_A:
            while d_next[0] < steps(d_stream):
                d_step()
            cross_wait(d_stream, 0)
            exchanged()
            panel_start()
        if u == PAN_X:
            panel_relay()
        if u == PAN_B:
            panel_pass()

    give(0).start()
    give(1).start()
    scatter_start(0)
    candidates()
    loads[2].wait()
    loads[3].wait()
    for i in range(2, zn):
        give(i).start()
    reduce_step(0)
    sources()
    for t in range(1, half):
        reduce_step(t)
        if SC_N < 15:
            scatter_start(t)
        if t >= D_START:
            d_step()
    give(zn - 1).wait_recv()
    for s in range(SUB):
        own_rows(s)
        if s == 0:
            ext_start()
    if D_MORE > 0:
        d_step()
    main = tuple(range(1, SUB + 1))
    gather_step(t_stream, 0, main)
    if D_MORE > 1:
        d_step()
    panel_point(0)
    ext_wait()
    gather_step(t_stream, 0, (0,))
    for u in range(1, steps(t_stream)):
        gather_step(t_stream, u, main + (0,))
        if D_MORE > 2:
            d_step()
        panel_point(u)
    cross_wait(t_stream, 0)
    panel_wait()

    lo0, lo1, up0, up1 = lo_ref[0], lo_ref[1], up_ref[0], up_ref[1]

    ext0 = te[0].reshape(block, block)
    ext1 = te[1].reshape(block, block)
    lower_t = dot(ext1, up0).astype(BF16)

    def top(s):
        cross_wait(t_stream, s + 1)
        t0 = tb[0, s].reshape(block, width)
        t1 = tb[1, s].reshape(block, width)
        return t0, t1, dot(lo0, t0).astype(BF16)

    def second(t1, u0):
        t1u = (t1.astype(F32) - dot(lower_t, u0)).astype(BF16)
        return t1u, dot(lo1, t1u).astype(BF16)

    @pl.when(row == 0)
    def _():
        for s in range(SUB):
            o_ref[:, cols(s)] = top(s)[2]

        @pl.when(col == 0)
        def _():
            o_ref[:, 0:block] = tb[0, 0].reshape(block, width)[:, 0:block]

    @pl.when(row == 1)
    def _():
        for s in range(SUB):
            _, t1, u0 = top(s)
            t1u, u1 = second(t1, u0)
            o_ref[:, cols(s)] = u1
            if s == 0:
                @pl.when(col == 1)
                def _():
                    o_ref[:, 0:block] = t1u[:, 0:block]

        @pl.when(col == 0)
        def _():
            o_ref[:, 0:block] = lower_t

    @pl.when(row > 1)
    def _():
        l0 = pb[0]
        u0e = dot(lo0, ext0).astype(BF16)
        y1 = (pb[1].astype(F32) - dot(l0, u0e)).astype(BF16)
        l1 = dot(y1, up1).astype(BF16)
        ll = jnp.concatenate([l0, l1], axis=1)
        for s in range(SUB):
            _, t1, u0 = top(s)
            _, u1 = second(t1, u0)
            uu = jnp.concatenate([u0, u1], axis=0)
            o_ref[:, cols(s)] = (o_ref[:, cols(s)].astype(F32) - dot(ll, uu)).astype(BF16)

        @pl.when(col == 0)
        def _():
            o_ref[:, 0:block] = l0

        @pl.when(col == 1)
        def _():
            o_ref[:, 0:block] = l1

    panel_far(lambda c: c.wait_send())
    panel_near(lambda c: c.wait_send(), 0)
    panel_near(lambda c: c.wait_send(), far)
    core_copy(0).wait_send()

    @pl.when(is_root)
    def _():
        for k in order:
            scatter_main(k).wait_send()

    gather_sent(d_stream)
    for i in range(zn):
        give(i).wait_send()
    for s in range(SUB):
        for t in range(half):
            plus(t, s).wait_send()
            if t < half - 1:
                minus(t, s).wait_send()
    ext(lambda c: c.wait_send())
    gather_sent(t_stream)


def pin(x):
    return pltpu.with_memory_space_constraint(x, pltpu.MemorySpace.HBM)


def body(matrix, pivots, lower_inverse, upper_inverse):
    local_rows, local_cols = matrix.shape
    block = lower_inverse.shape[1]
    rows_n = lax.axis_size("row")
    cols_n = lax.axis_size("col")
    zn = rows_n // 2
    half = zn // 2
    per = block // zn
    width = local_cols // SUB
    sem = pltpu.SemaphoreType.DMA
    vmem = pltpu.VMEM
    tn = SUB + 1
    return pl.pallas_call(
        functools.partial(kernel, rows_n, cols_n),
        out_shape=jax.ShapeDtypeStruct((local_rows, local_cols), BF16),
        in_specs=[
            pl.BlockSpec(memory_space=pltpu.MemorySpace.HBM),
            pl.BlockSpec(memory_space=pltpu.MemorySpace.HBM),
            pl.BlockSpec(memory_space=pltpu.MemorySpace.HBM),
            pl.BlockSpec(memory_space=pltpu.MemorySpace.HBM),
        ],
        out_specs=pl.BlockSpec(memory_space=pltpu.VMEM),
        scratch_shapes=[
            vmem(pivots.shape, jnp.int32),
            vmem((local_rows, local_cols), BF16),
            vmem(lower_inverse.shape, BF16),
            vmem(upper_inverse.shape, BF16),
            sem((4,)),
            vmem((zn, 2, SUB, per, width), BF16),
            vmem((2, 2, SUB, per, width), BF16),
            vmem((zn, 2, per, block), BF16),
            vmem((half, SUB, per, width), BF16),
            vmem((half - 1, SUB, per, width), BF16),
            vmem((zn, SUB, per, width), BF16),
            vmem((2, SUB, zn, per, width), BF16),
            vmem((2, zn, per, block), BF16),
            vmem((2, zn, per, local_cols), BF16),
            vmem((2, block, block), BF16),
            vmem((block, 2 * block), BF16),
            vmem((block, 128), F32),
            sem((half, SUB)), sem((half, SUB)),
            sem((half - 1, SUB)), sem((half - 1, SUB)),
            sem((zn,)), sem((zn,)),
            sem((cols_n,)), sem(()),
            sem((2 * half, tn)), sem((2 * half, tn)),
            sem((2 * half, tn)), sem((2 * half, tn)),
            sem((2 * half, 1)), sem((2 * half, 1)),
            sem((2 * half, 1)), sem((2 * half, 1)),
            sem((cols_n,)), sem((2,)),
            sem((zn,)), sem(()),
        ],
        compiler_params=pltpu.CompilerParams(
            collective_id=0, has_side_effects=True, vmem_limit_bytes=VLIM << 20
        ),
    )(pin(matrix), pin(pivots), pin(lower_inverse), pin(upper_inverse))


def solution(mesh):
    placed = (P("row", "col"), P(), P(), P())
    return jax.shard_map(
        body, mesh=mesh, in_specs=placed, out_specs=P("row", "col"), check_vma=False
    )
```
